32 devices in a mesh: atm: 4 (over y, x), ocn: 8 (over z, core).
Axes of the slice: x: 2, y: 2, z: 4, core: 2. Of those that a mesh axis runs over, the one named last changes fastest.
Arguments:
- atm_flux: float32 [8, 221184], P(None, ('atm', 'ocn')), may hold values from -6 to 6
- send_cell: int32 [32, 32, 512], P(('atm', 'ocn')), may hold values from 0 to 6911, as said below
- send_weight: float32 [32, 32, 512], P(('atm', 'ocn')), may hold values from 0 to 1, as said below
- recv_cell: int32 [32, 32, 512], P(('atm', 'ocn')), may hold values from 0 to 8191, as said below
- temp: float32 [20, 128, 2048], P(None, 'ocn', 'atm'), may hold values from -6 to 6
- salt: float32 [20, 128, 2048], P(None, 'ocn', 'atm'), may hold values from -6 to 6
- uvel: float32 [20, 128, 2048], P(None, 'ocn', 'atm'), may hold values from -4 to 4
- vvel: float32 [20, 128, 2048], P(None, 'ocn', 'atm'), may hold values from -4 to 4
- wet_mask: int32 [128, 2048], P('ocn', 'atm'), may hold values 0 or 1
- vert_mix: float32 [19, 128, 2048], P(None, 'ocn', 'atm'), may hold values from 0.05 to 5
Outputs:
- temp_out: float32 [20, 128, 2048], P(None, 'ocn', 'atm')
- salt_out: float32 [20, 128, 2048], P(None, 'ocn', 'atm')
- uvel_out: float32 [20, 128, 2048], P(None, 'ocn', 'atm')
- vvel_out: float32 [20, 128, 2048], P(None, 'ocn', 'atm')
- atm_surface: float32 [4, 221184], P(None, ('atm', 'ocn'))
The draws below stay inside these ranges and needn't reach their ends.
Inputs may be any that keep to these rules, and one draw needn't show every extreme that they name: Slot c of send_cell[s, d], send_weight[s, d] and recv_cell[d, s] is one intersection between a cell of source device s and a cell of destination device d. Each pair of devices uses a leading run of 128 to 512 slots; one destination device receives all 512 slots from every source. Empty slots hold cell 0 and weight 0. `recv_cell`: local ocean cell numbers, as described for send_cell. `send_weight`: zero exactly in empty slots, else at least 0.02.
All inputs are finite; a program needn't handle non-finite values. No bound on the sum of `wet_mask` on one device may be relied on, other than what follows from the above.
Results may differ from the reference program's by a relative error of at most 0.00002.
Values sent between devices are 32-bit elements; how exact they have to be, the bound alone decides.
No kernel may reach another device: no remote copies, remote signals or barrier semaphores. Data moves between devices by JAX's collectives and lax.ppermute only.
A program may use at most 128 MiB of HBM per device.

```python
import math
import jax
import jax.numpy as jnp
from jax import lax

NFLUX = 8
LEV = 20
STEPS = 2
OJ = 16
OI = 512
ACELL_DEV = 6912
CAP = 512
NJ = 128
NI = 2048
ACELLS = 221184
N_OCN = 8
DEVICES = 32


def intersection_plan(key):
    fill_count = jax.random.randint(jax.random.fold_in(key, 101), (DEVICES, DEVICES), CAP // 4, CAP + 1)
    full_dest = jax.random.randint(jax.random.fold_in(key, 102), (), 0, DEVICES)
    dest_ids = jnp.arange(DEVICES)[None, :]
    fill_count = jnp.where(dest_ids == full_dest, CAP, fill_count)
    slot_ids = jnp.arange(CAP)[None, None, :]
    occupied = slot_ids < fill_count[:, :, None]
    source_ids = jnp.arange(DEVICES)[:, None, None]
    corner_slot = (source_ids == 0) & (dest_ids[:, :, None] == full_dest) & (slot_ids == 0)
    source_cells = jax.random.randint(jax.random.fold_in(key, 103), (DEVICES, DEVICES, CAP), 0, ACELL_DEV)
    source_cells = jnp.where(corner_slot, ACELL_DEV - 1, source_cells)
    ocean_cells = jax.random.randint(jax.random.fold_in(key, 104), (DEVICES, DEVICES, CAP), 0, OJ * OI)
    ocean_cells = jnp.where(corner_slot, OJ * OI - 1, ocean_cells)
    source_cells = jnp.where(occupied, source_cells, 0)
    ocean_cells = jnp.where(occupied, ocean_cells, 0)
    return (occupied, source_cells, ocean_cells)


def draw_send_cell(key, part):
    return intersection_plan(key)[1].astype(jnp.int32)


def draw_recv_cell(key, part):
    return jnp.transpose(intersection_plan(key)[2], (1, 0, 2)).astype(jnp.int32)


def draw_send_weight(key, part):
    occupied = intersection_plan(key)[0]
    values_drawn = jnp.exp(jax.random.uniform(jax.random.fold_in(key, 106), (DEVICES, DEVICES, CAP), jnp.float32, jnp.log(0.02), 0.0))
    return jnp.where(occupied, values_drawn, 0.0).astype(jnp.float32)


def touch_ends(entries, stream_key, smallest, largest):
    dims = entries.shape
    index_at = [jax.random.randint(jax.random.fold_in(stream_key, axis), (), 0, dims[axis]) for axis in range(len(dims))]
    entries = entries.at[tuple(index_at)].set(smallest)
    longest = dims.index(max(dims))
    index_at[longest] = (index_at[longest] + 1) % dims[longest]
    return entries.at[tuple(index_at)].set(largest)


def shard_levels(rng, dims, split, low, high):
    factor_of, own = 1.0, jax.random.fold_in(rng, 6)
    for axis_at, shards_of in split:
        steps = jnp.exp(jax.random.uniform(jax.random.fold_in(own, axis_at), (shards_of,), jnp.float32, low / len(split), high / len(split)))
        factor_of = factor_of * jnp.repeat(steps, dims[axis_at] // shards_of).reshape([-1 if axis == axis_at else 1 for axis in range(len(dims))])
    return factor_of


def scatter_about(own_key, shape, width, reach, cuts=(), held_as=jnp.bfloat16):
    values = jax.random.normal(own_key, shape, jnp.float32) * width
    if len(cuts) > 0:
        values = shard_levels(own_key, shape, cuts, -0.22, 0.18) * values
    return jnp.clip(values, min=-reach, max=reach).astype(held_as)


def setup_inputs(seed: int = 0) -> dict:
    seeds = jax.random.split(jax.random.key(seed), 11)
    return {
        "atm_flux": scatter_about(seeds[0], (NFLUX, ACELLS), 1.0, 6.0, ((1, 32),), jnp.float32),
        "send_cell": draw_send_cell(jax.random.fold_in(seeds[10], 71), 0),
        "send_weight": draw_send_weight(jax.random.fold_in(seeds[10], 71), 0),
        "recv_cell": draw_recv_cell(jax.random.fold_in(seeds[10], 71), 0),
        "temp": scatter_about(seeds[4], (LEV, NJ, NI), 1.0, 6.0, ((1, 8), (2, 4)), jnp.float32),
        "salt": scatter_about(seeds[5], (LEV, NJ, NI), 1.0, 6.0, ((1, 8), (2, 4)), jnp.float32),
        "uvel": scatter_about(seeds[6], (LEV, NJ, NI), 1.0, 4.0, ((1, 8), (2, 4)), jnp.float32),
        "vvel": scatter_about(seeds[7], (LEV, NJ, NI), 1.0, 4.0, ((1, 8), (2, 4)), jnp.float32),
        "wet_mask": touch_ends((jax.random.randint(seeds[8], (NJ, NI), 0, 5) < 3).astype(jnp.int32), jax.random.fold_in(seeds[8], 1), 0, 1),
        "vert_mix": jnp.clip(jnp.exp(math.log(5.0) - 4.6051702 * jax.random.uniform(seeds[9], (LEV - 1, NJ, NI), jnp.float32) ** shard_levels(seeds[9], (LEV - 1, NJ, NI), ((1, 8), (2, 4)), -0.2, 0.2)), 0.05, 5.0),
    }


courant_scale = 0.05
diffusion = 0.15
viscosity = 0.15
coriolis = 0.1
heat_gain = 0.25
water_gain = 0.25
stress_gain = 0.25


def make_sign(levels):
    return jnp.concatenate([jnp.ones((2 * levels,), jnp.float32), -jnp.ones((2 * levels,), jnp.float32), jnp.ones((1,), jnp.float32)])


def coriolis_profile(row_ids, total_rows):
    mirrored = jnp.where(row_ids >= total_rows, 2 * total_rows - 1 - row_ids, row_ids)
    latitude = jnp.pi * ((mirrored.astype(jnp.float32) + 0.5) / total_rows - 0.5)
    return (coriolis * jnp.sin(latitude))[:, None]


def tendency(centre, east_cells, west_cells, north_cells, south_cells, coriolis_rows, levels):
    wet_cells = centre[-1]
    gate_east = east_cells[-1] * wet_cells
    gate_west = west_cells[-1] * wet_cells
    gate_north = north_cells[-1] * wet_cells
    gate_south = south_cells[-1] * wet_cells
    fields = centre[:-1]
    diff_east = gate_east * (east_cells[:-1] - fields)
    diff_west = gate_west * (fields - west_cells[:-1])
    diff_north = gate_north * (north_cells[:-1] - fields)
    diff_south = gate_south * (fields - south_cells[:-1])
    laplace = diff_east - diff_west + diff_north - diff_south
    plane_shape = fields.shape[1:]
    velocity_east = fields[2 * levels:3 * levels]
    velocity_north = fields[3 * levels:4 * levels]
    courant_east = courant_scale * velocity_east
    courant_north = courant_scale * velocity_north

    def tracer_part(values_in):
        return values_in[:2 * levels].reshape((2, levels) + plane_shape)

    upwind = (jnp.maximum(courant_east, 0.0) * tracer_part(diff_west) + jnp.minimum(courant_east, 0.0) * tracer_part(diff_east)
              + jnp.maximum(courant_north, 0.0) * tracer_part(diff_south) + jnp.minimum(courant_north, 0.0) * tracer_part(diff_north))
    tracers = tracer_part(fields) + wet_cells * (diffusion * tracer_part(laplace) - upwind)
    east_next = velocity_east + wet_cells * (viscosity * laplace[2 * levels:3 * levels] + coriolis_rows * velocity_north)
    north_next = velocity_north + wet_cells * (viscosity * laplace[3 * levels:4 * levels] - coriolis_rows * velocity_east)
    return jnp.concatenate([tracers.reshape((2 * levels,) + plane_shape), east_next, north_next, centre[-1:]], 0)


def surface_forcing(flux):
    heat_flux = flux[0] + flux[1] + flux[2] + flux[3]
    water_flux = flux[4] - flux[5]
    return jnp.stack([heat_gain * heat_flux, water_gain * water_flux, stress_gain * flux[6], stress_gain * flux[7]])


def force(fields, flux, wet_cells):
    return fields.at[:, 0].add(surface_forcing(flux) * wet_cells)


def vertical_solve(fields, mixing):
    levels = fields.shape[1]
    factors = []
    partial_rows = []
    for level_index in range(levels):
        upper_mix = mixing[level_index - 1] if level_index > 0 else jnp.zeros_like(mixing[0])
        lower_mix = mixing[level_index] if level_index < levels - 1 else jnp.zeros_like(mixing[0])
        diagonal = 1.0 + upper_mix + lower_mix
        if level_index == 0:
            pivot_value = diagonal
            right_side = fields[:, 0]
        else:
            pivot_value = diagonal + upper_mix * factors[-1]
            right_side = fields[:, level_index] + upper_mix * partial_rows[-1]
        factors.append(-lower_mix / pivot_value)
        partial_rows.append(right_side / pivot_value)
    solved = [partial_rows[-1]]
    for level_index in range(levels - 2, -1, -1):
        solved.append(partial_rows[level_index] - factors[level_index] * solved[-1])
    return jnp.stack(solved[::-1], 1)


def reference(atm_flux, send_cell, send_weight, recv_cell, temp, salt, uvel, vvel, wet_mask, vert_mix):
    levels = temp.shape[0]
    wet_cells = wet_mask.astype(jnp.float32)
    dest_ids = jnp.arange(DEVICES, dtype=jnp.int32)[:, None, None]
    ocean_index = ((dest_ids % N_OCN) * OJ + recv_cell // OI) * NI + (dest_ids // N_OCN) * OI + recv_cell % OI
    source_ids = jnp.arange(DEVICES, dtype=jnp.int32)

    def forward(totals, source_index):
        slot_cells = lax.dynamic_index_in_dim(send_cell, source_index, 0, keepdims=False)
        slot_weights = lax.dynamic_index_in_dim(send_weight, source_index, 0, keepdims=False)
        outgoing = jnp.take(atm_flux, (source_index * ACELL_DEV + slot_cells).reshape(-1), axis=1).reshape(NFLUX, DEVICES, CAP) * slot_weights[None]
        targets = lax.dynamic_index_in_dim(ocean_index, source_index, 1, keepdims=False)
        return totals.at[:, targets.reshape(-1)].add(outgoing.reshape(NFLUX, -1)), None

    ocean_flux = lax.scan(forward, jnp.zeros((NFLUX, NJ * NI), jnp.float32), source_ids)[0].reshape(NFLUX, NJ, NI)

    state_stack = jnp.concatenate([temp, salt, uvel, vvel, wet_cells[None]], 0)
    fold_sign = make_sign(levels)
    coriolis_rows = coriolis_profile(jnp.arange(NJ, dtype=jnp.int32), NJ)
    for step_index in range(STEPS):
        north_ghost = state_stack[:, NJ - 1:, ::-1] * fold_sign[:, None, None]
        north_cells = jnp.concatenate([state_stack[:, 1:], north_ghost], 1)
        south_cells = jnp.concatenate([jnp.zeros_like(state_stack[:, :1]), state_stack[:, :-1]], 1)
        state_stack = tendency(state_stack, jnp.roll(state_stack, -1, 2), jnp.roll(state_stack, 1, 2), north_cells, south_cells, coriolis_rows, levels)

    fields = state_stack[:4 * levels].reshape(4, levels, NJ, NI)
    fields = force(fields, ocean_flux, wet_cells)
    fields = vertical_solve(fields, vert_mix)
    surface = fields[:, 0].reshape(4, NJ * NI)

    def backward(totals, source_index):
        slot_cells = lax.dynamic_index_in_dim(send_cell, source_index, 0, keepdims=False)
        slot_weights = lax.dynamic_index_in_dim(send_weight, source_index, 0, keepdims=False)
        targets = lax.dynamic_index_in_dim(ocean_index, source_index, 1, keepdims=False)
        returning = jnp.take(surface, targets.reshape(-1), axis=1).reshape(4, DEVICES, CAP) * slot_weights[None]
        return totals.at[:, (source_index * ACELL_DEV + slot_cells).reshape(-1)].add(returning.reshape(4, -1)), None

    gathered_sum = lax.scan(backward, jnp.zeros((4, ACELLS), jnp.float32), source_ids)[0]
    weight_total = jnp.zeros((ACELLS,), jnp.float32).at[(source_ids[:, None, None] * ACELL_DEV + send_cell).reshape(-1)].add(send_weight.reshape(-1))
    atm_surface = gathered_sum / jnp.maximum(weight_total, 1.0)
    return fields[0], fields[1], fields[2], fields[3], atm_surface
```

```python
import jax
import jax.numpy as jnp
from jax import lax
from jax.experimental import pallas as pl
from jax.experimental.pallas import tpu as pltpu
from jax.sharding import PartitionSpec as P

STEPS = 2


LANES = 256
TERMS = 3
GROUP = 8


def cut(values):
    terms = []
    rest = values
    for term_index in range(TERMS):
        term = rest.astype(jnp.bfloat16)
        terms.append(term)
        if term_index < TERMS - 1:
            rest = rest - term.astype(jnp.float32)
    return terms


def one_hot(positions, count):
    slots = positions.shape[1]
    base = positions - lax.broadcasted_iota(jnp.int32, (8, slots), 0)
    rows = [jnp.where(base == 8 * j, 1.0, 0.0) for j in range(count // 8)]
    return jnp.concatenate(rows, 0).astype(jnp.bfloat16)


def each_owner(owners, body):
    def outer(group, carry):
        body(group)
        return carry

    lax.fori_loop(0, owners // GROUP, outer, 0)


def send_kernel(flux_ref, cell_ref, weight_ref, out_ref, raw_ref, table_ref):
    owners, slots = cell_ref.shape
    blocks = flux_ref.shape[1] // LANES
    raw_ref[...] = jnp.zeros_like(raw_ref)
    for block in range(blocks):
        x = flux_ref[:, block * LANES : (block + 1) * LANES]
        heat = heat_gain * (x[0:1] + x[1:2] + x[2:3] + x[3:4])
        water = water_gain * (x[4:5] - x[5:6])
        raw_ref[4 * block : 4 * block + 4, :] = jnp.concatenate(
            [heat, water, stress_gain * x[6:8]], 0
        )
    rows = raw_ref.shape[0]
    for term_index, term in enumerate(cut(raw_ref[...])):
        table_ref[term_index * rows : (term_index + 1) * rows, :] = term

    def body(group):
        first = pl.multiple_of(group * GROUP, GROUP)
        cells = cell_ref[pl.ds(first, GROUP), :]
        weights = weight_ref[pl.ds(first, GROUP), :]
        for k in range(GROUP):
            cell = cells[k : k + 1]
            found = jnp.dot(
                table_ref[...],
                one_hot(cell & (LANES - 1), LANES),
                preferred_element_type=jnp.float32,
            )
            base = cell // LANES - lax.broadcasted_iota(jnp.int32, (8, slots), 0) // 4
            total = jnp.zeros((8, slots), jnp.float32)
            for j in range(rows // 8):
                value = found[8 * j : 8 * j + 8]
                for t in range(1, TERMS):
                    value = value + found[t * rows + 8 * j : t * rows + 8 * j + 8]
                total = total + jnp.where(base == 2 * j, value, 0.0)
            out_ref[first + k] = (total[0:4] + total[4:8]) * weights[k : k + 1]

    each_owner(owners, body)


def collect_kernel(come_ref, cell_ref, out_ref, sum_ref):
    owners, slots = cell_ref.shape
    rows, cols = out_ref.shape[1:]
    high = rows * cols // LANES
    sum_ref[...] = jnp.zeros_like(sum_ref)

    def body(group):
        first = pl.multiple_of(group * GROUP, GROUP)
        cells = cell_ref[pl.ds(first, GROUP), :]
        for k in range(GROUP):
            cell = cells[k : k + 1]
            col = cell % cols
            spot = (col // LANES) * rows + cell // cols
            mask = lax.broadcasted_iota(jnp.int32, (high, slots), 0) == spot
            left = []
            for term in cut(come_ref[first + k]):
                wide = term.astype(jnp.float32)
                for f in range(4):
                    left.append(jnp.where(mask, wide[f : f + 1], 0.0))
            sum_ref[...] += lax.dot_general(
                jnp.concatenate(left, 0).astype(jnp.bfloat16),
                one_hot(col % LANES, LANES),
                (((1,), (1,)), ((), ())),
                preferred_element_type=jnp.float32,
            )

    each_owner(owners, body)
    for f in range(4):
        for b in range(cols // LANES):
            value = 0.0
            for t in reversed(range(TERMS)):
                at = (t * 4 + f) * high + b * rows
                value = value + sum_ref[at : at + rows, :]
            out_ref[f, :, b * LANES : (b + 1) * LANES] = value


def surface_kernel(surface_ref, cell_ref, out_ref, table_ref):
    owners, slots = cell_ref.shape
    rows, cols = surface_ref.shape[1:]
    high = rows * cols // LANES
    for f in range(4):
        for b in range(cols // LANES):
            part = surface_ref[f, :, b * LANES : (b + 1) * LANES]
            for t, term in enumerate(cut(part)):
                at = (t * 4 + f) * high + b * rows
                table_ref[at : at + rows, :] = term

    def body(group):
        first = pl.multiple_of(group * GROUP, GROUP)
        cells = cell_ref[pl.ds(first, GROUP), :]
        for k in range(GROUP):
            cell = cells[k : k + 1]
            col = cell % cols
            spot = (col // LANES) * rows + cell // cols
            found = jnp.dot(
                table_ref[...],
                one_hot(col % LANES, LANES),
                preferred_element_type=jnp.float32,
            )
            base = spot - lax.broadcasted_iota(jnp.int32, (8, slots), 0)
            masks = [base == 8 * j for j in range(high // 8)]
            picked = []
            for f in range(4):
                total = jnp.zeros((8, slots), jnp.float32)
                for j in range(high // 8):
                    at = f * high + 8 * j
                    value = found[at : at + 8]
                    for t in range(1, TERMS):
                        value = value + found[t * 4 * high + at : t * 4 * high + at + 8]
                    total = total + jnp.where(masks[j], value, 0.0)
                picked.append(jnp.sum(total, axis=0, keepdims=True))
            out_ref[first + k] = jnp.concatenate(picked, 0)

    each_owner(owners, body)


def weight_kernel(cell_ref, weight_ref, out_ref, sum_ref):
    owners, slots = cell_ref.shape
    high = sum_ref.shape[0] // TERMS
    sum_ref[...] = jnp.zeros_like(sum_ref)

    def body(group):
        first = pl.multiple_of(group * GROUP, GROUP)
        cells = cell_ref[pl.ds(first, GROUP), :]
        weights = weight_ref[pl.ds(first, GROUP), :]
        for k in range(GROUP):
            cell = cells[k : k + 1]
            mask = lax.broadcasted_iota(jnp.int32, (high, slots), 0) == cell // LANES
            left = [
                jnp.where(mask, term.astype(jnp.float32), 0.0)
                for term in cut(weights[k : k + 1])
            ]
            sum_ref[...] += lax.dot_general(
                jnp.concatenate(left, 0).astype(jnp.bfloat16),
                one_hot(cell & (LANES - 1), LANES),
                (((1,), (1,)), ((), ())),
                preferred_element_type=jnp.float32,
            )

    each_owner(owners, body)
    value = 0.0
    for t in reversed(range(TERMS)):
        value = value + sum_ref[t * high : (t + 1) * high, :]
    out_ref[...] = 1.0 / jnp.maximum(value, 1.0)


def return_kernel(come_ref, cell_ref, weight_ref, inverse_ref, out_ref, sum_ref):
    owners, slots = cell_ref.shape
    blocks = out_ref.shape[1] // LANES
    rows = sum_ref.shape[0] // TERMS
    sum_ref[...] = jnp.zeros_like(sum_ref)

    def body(group):
        first = pl.multiple_of(group * GROUP, GROUP)
        cells = cell_ref[pl.ds(first, GROUP), :]
        weights = weight_ref[pl.ds(first, GROUP), :]
        for k in range(GROUP):
            cell = cells[k : k + 1]
            base = cell // LANES - lax.broadcasted_iota(jnp.int32, (8, slots), 0) // 4
            left = []
            for term in cut(come_ref[first + k] * weights[k : k + 1]):
                wide = term.astype(jnp.float32)
                wide = jnp.concatenate([wide, wide], 0)
                for j in range(rows // 8):
                    left.append(jnp.where(base == 2 * j, wide, 0.0))
            sum_ref[...] += lax.dot_general(
                jnp.concatenate(left, 0).astype(jnp.bfloat16),
                one_hot(cell & (LANES - 1), LANES),
                (((1,), (1,)), ((), ())),
                preferred_element_type=jnp.float32,
            )

    each_owner(owners, body)
    for block in range(blocks):
        value = 0.0
        for t in reversed(range(TERMS)):
            at = t * rows + 4 * block
            value = value + sum_ref[at : at + 4, :]
        out_ref[:, block * LANES : (block + 1) * LANES] = (
            value * inverse_ref[block : block + 1, :]
        )


def up_to(count, step):
    return (count + step - 1) // step * step


def call(kernel, out_shape, scratch, *operands):
    return pl.pallas_call(
        kernel,
        out_shape=jax.ShapeDtypeStruct(out_shape, jnp.float32),
        scratch_shapes=[pltpu.VMEM(shape, dtype) for shape, dtype in scratch],
        compiler_params=pltpu.CompilerParams(vmem_limit_bytes=40 * 2**20),
    )(*operands)


courant_scale = 0.05
diffusion = 0.15
viscosity = 0.15
coriolis = 0.1
heat_gain = 0.25
water_gain = 0.25
stress_gain = 0.25


def partner(block, axis, distance):
    count = lax.axis_size(axis)
    route = []
    for low in range(count):
        high = low | 1 << distance
        if high != low and high < count:
            route += [(low, high), (high, low)]
    return lax.ppermute(block, axis, route)


def padded(cells, sides, width, closed):
    for axis, dim in sides:
        count = lax.axis_size(axis)
        ends = count if closed else count - 1
        head = lax.slice_in_dim(cells, 0, width, axis=dim)
        tail = lax.slice_in_dim(cells, cells.shape[dim] - width, cells.shape[dim], axis=dim)
        cells = jnp.concatenate(
            [
                lax.ppermute(tail, axis, [(i, (i + 1) % count) for i in range(ends)]),
                cells,
                lax.ppermute(head, axis, [((i + 1) % count, i) for i in range(ends)]),
            ],
            axis=dim,
        )
    return cells


def make_sign(levels):
    return jnp.concatenate(
        [
            jnp.ones((2 * levels,), jnp.float32),
            -jnp.ones((2 * levels,), jnp.float32),
            jnp.ones((1,), jnp.float32),
        ]
    )


def coriolis_profile(row_ids, total_rows):
    mirrored = jnp.where(row_ids >= total_rows, 2 * total_rows - 1 - row_ids, row_ids)
    latitude = jnp.pi * ((mirrored.astype(jnp.float32) + 0.5) / total_rows - 0.5)
    return (coriolis * jnp.sin(latitude))[:, None]


def tendency(centre, east_cells, west_cells, north_cells, south_cells, coriolis_rows, levels):
    wet_cells = centre[-1]
    gate_east = east_cells[-1] * wet_cells
    gate_west = west_cells[-1] * wet_cells
    gate_north = north_cells[-1] * wet_cells
    gate_south = south_cells[-1] * wet_cells
    fields = centre[:-1]
    diff_east = gate_east * (east_cells[:-1] - fields)
    diff_west = gate_west * (fields - west_cells[:-1])
    diff_north = gate_north * (north_cells[:-1] - fields)
    diff_south = gate_south * (fields - south_cells[:-1])
    laplace = diff_east - diff_west + diff_north - diff_south
    plane_shape = fields.shape[1:]
    velocity_east = fields[2 * levels : 3 * levels]
    velocity_north = fields[3 * levels : 4 * levels]
    courant_east = courant_scale * velocity_east
    courant_north = courant_scale * velocity_north

    def tracer_part(values_in):
        return values_in[: 2 * levels].reshape((2, levels) + plane_shape)

    upwind = (
        jnp.maximum(courant_east, 0.0) * tracer_part(diff_west)
        + jnp.minimum(courant_east, 0.0) * tracer_part(diff_east)
        + jnp.maximum(courant_north, 0.0) * tracer_part(diff_south)
        + jnp.minimum(courant_north, 0.0) * tracer_part(diff_north)
    )
    tracers = tracer_part(fields) + wet_cells * (diffusion * tracer_part(laplace) - upwind)
    east_next = velocity_east + wet_cells * (
        viscosity * laplace[2 * levels : 3 * levels] + coriolis_rows * velocity_north
    )
    north_next = velocity_north + wet_cells * (
        viscosity * laplace[3 * levels : 4 * levels] - coriolis_rows * velocity_east
    )
    return jnp.concatenate(
        [tracers.reshape((2 * levels,) + plane_shape), east_next, north_next, centre[-1:]], 0
    )


def vertical_solve(fields, mixing):
    levels = fields.shape[1]
    factors = []
    partial_rows = []
    for level_index in range(levels):
        upper_mix = mixing[level_index - 1] if level_index > 0 else jnp.zeros_like(mixing[0])
        lower_mix = mixing[level_index] if level_index < levels - 1 else jnp.zeros_like(mixing[0])
        diagonal = 1.0 + upper_mix + lower_mix
        if level_index == 0:
            pivot_value = diagonal
            right_side = fields[:, 0]
        else:
            pivot_value = diagonal + upper_mix * factors[-1]
            right_side = fields[:, level_index] + upper_mix * partial_rows[-1]
        factors.append(-lower_mix / pivot_value)
        partial_rows.append(right_side / pivot_value)
    solved = [partial_rows[-1]]
    for level_index in range(levels - 2, -1, -1):
        solved.append(partial_rows[level_index] - factors[level_index] * solved[-1])
    return jnp.stack(solved[::-1], 1)


def mirror_partner(top_rows):
    mirrored = top_rows
    for bit_number in range(lax.axis_size("atm").bit_length() - 1):
        mirrored = partner(mirrored, "atm", bit_number)
    return mirrored


def extend(state_stack, margin_width, fold_sign):
    widened = padded(state_stack, (("atm", 2),), margin_width, True)
    top_rows = widened[:, widened.shape[1] - margin_width :, :]
    ghost_rows = mirror_partner(top_rows)[:, ::-1, ::-1] * fold_sign[:, None, None]
    heightened = padded(widened, (("ocn", 1),), margin_width, False)
    split_at = heightened.shape[1] - margin_width
    on_top = lax.axis_index("ocn") == lax.axis_size("ocn") - 1
    upper_rows = jnp.where(on_top, ghost_rows, heightened[:, split_at:, :])
    return jnp.concatenate([heightened[:, :split_at, :], upper_rows], 1)


def advance(extended, first_row, levels, block_rows):
    row_count = extended.shape[1] - 2
    row_ids = (
        lax.axis_index("ocn") * block_rows + first_row + jnp.arange(row_count, dtype=jnp.int32)
    )
    coriolis_rows = coriolis_profile(row_ids, block_rows * lax.axis_size("ocn"))
    return tendency(
        extended[:, 1:-1, 1:-1],
        extended[:, 1:-1, 2:],
        extended[:, 1:-1, :-2],
        extended[:, 2:, 1:-1],
        extended[:, :-2, 1:-1],
        coriolis_rows,
        levels,
    )


def per_device(
    atm_flux, send_cell, send_weight, recv_cell, temp, salt, uvel, vvel, wet_mask, vert_mix
):
    levels, block_rows, block_cols = temp.shape
    slot_cells = send_cell[0]
    slot_weights = send_weight[0]
    arrival_cells = recv_cell[0]
    owners, capacity = slot_cells.shape
    atm_cells = atm_flux.shape[1]
    blocks = atm_cells // LANES
    rows = up_to(4 * blocks, 16)
    high = block_rows * block_cols // LANES
    outgoing = call(
        send_kernel,
        (owners, 4, capacity),
        [((rows, LANES), jnp.float32), ((TERMS * rows, LANES), jnp.bfloat16)],
        atm_flux,
        slot_cells,
        slot_weights,
    )
    incoming = lax.all_to_all(outgoing, ("atm", "ocn"), split_axis=0, concat_axis=0, tiled=True)
    inverse = call(
        weight_kernel,
        (up_to(blocks, 16), LANES),
        [((TERMS * up_to(blocks, 16), LANES), jnp.float32)],
        slot_cells,
        slot_weights,
    )
    push = call(
        collect_kernel,
        (4, block_rows, block_cols),
        [((TERMS * 4 * high, LANES), jnp.float32)],
        incoming,
        arrival_cells,
    )
    wet_cells = wet_mask.astype(jnp.float32)
    state_stack = jnp.concatenate([temp, salt, uvel, vvel, wet_cells[None]], 0)
    fold_sign = make_sign(levels)
    for step_index in range(STEPS):
        state_stack = advance(extend(state_stack, 1, fold_sign), 0, levels, block_rows)
    fields = state_stack[: 4 * levels].reshape(4, levels, block_rows, block_cols)
    fields = fields.at[:, 0].add(push * wet_cells)
    fields = vertical_solve(fields, vert_mix)
    leaving = call(
        surface_kernel,
        (owners, 4, capacity),
        [((TERMS * 4 * high, LANES), jnp.bfloat16)],
        fields[:, 0],
        arrival_cells,
    )
    returning = lax.all_to_all(leaving, ("atm", "ocn"), split_axis=0, concat_axis=0, tiled=True)
    atm_surface = call(
        return_kernel,
        (4, atm_cells),
        [((TERMS * rows, LANES), jnp.float32)],
        returning,
        slot_cells,
        slot_weights,
        inverse,
    )
    return (fields[0], fields[1], fields[2], fields[3], atm_surface)


def solution(mesh):
    in_specs = (
        P(None, ("atm", "ocn")),
        P(("atm", "ocn"), None, None),
        P(("atm", "ocn"), None, None),
        P(("atm", "ocn"), None, None),
        P(None, "ocn", "atm"),
        P(None, "ocn", "atm"),
        P(None, "ocn", "atm"),
        P(None, "ocn", "atm"),
        P("ocn", "atm"),
        P(None, "ocn", "atm"),
    )
    out_specs = (
        P(None, "ocn", "atm"),
        P(None, "ocn", "atm"),
        P(None, "ocn", "atm"),
        P(None, "ocn", "atm"),
        P(None, ("atm", "ocn")),
    )
    return jax.shard_map(
        per_device, mesh=mesh, in_specs=in_specs, out_specs=out_specs, check_vma=False
    )
```

```python
import functools
import math

import jax
import jax.numpy as jnp
from jax import lax
from jax.experimental import pallas as pl
from jax.experimental.pallas import tpu as pltpu
from jax.sharding import PartitionSpec as P

courant_scale = 0.05
diffusion = 0.15
viscosity = 0.15
coriolis = 0.1
heat_gain = 0.25
water_gain = 0.25
stress_gain = 0.25


LANES = 256
TERMS = 3
GROUP = 8
VMEM_BYTES = 60 * 2**20
SMALL_BYTES = 24 * 2**20


def cut(values):
    terms = []
    rest = values
    for term_index in range(TERMS):
        term = rest.astype(jnp.bfloat16)
        terms.append(term)
        if term_index < TERMS - 1:
            rest = rest - term.astype(jnp.float32)
    return terms


def one_hot(positions, count):
    slots = positions.shape[1]
    base = positions - lax.broadcasted_iota(jnp.int32, (8, slots), 0)
    rows = [jnp.where(base == 8 * j, 1.0, 0.0) for j in range(count // 8)]
    return jnp.concatenate(rows, 0).astype(jnp.bfloat16)


def each_owner(owners, body):
    def outer(group, carry):
        body(group)
        return carry

    lax.fori_loop(0, owners // GROUP, outer, 0)


def send_kernel(
    flux_in, cell_in, weight_in, out_ref, flux_ref, cell_ref, weight_ref, raw_ref, table_ref, sem
):
    owners, slots = cell_ref.shape
    copies = [
        pltpu.make_async_copy(flux_in, flux_ref, sem.at[0]),
        pltpu.make_async_copy(cell_in, cell_ref, sem.at[1]),
        pltpu.make_async_copy(weight_in, weight_ref, sem.at[2]),
    ]
    for copy in copies:
        copy.start()
    blocks = flux_ref.shape[1] // LANES
    raw_ref[...] = jnp.zeros_like(raw_ref)
    copies[0].wait()
    for block in range(blocks):
        x = flux_ref[:, block * LANES : (block + 1) * LANES]
        heat = heat_gain * (x[0:1] + x[1:2] + x[2:3] + x[3:4])
        water = water_gain * (x[4:5] - x[5:6])
        raw_ref[4 * block : 4 * block + 4, :] = jnp.concatenate(
            [heat, water, stress_gain * x[6:8]], 0
        )
    rows = raw_ref.shape[0]
    for term_index, term in enumerate(cut(raw_ref[...])):
        table_ref[term_index * rows : (term_index + 1) * rows, :] = term
    copies[1].wait()
    copies[2].wait()

    def body(group):
        first = pl.multiple_of(group * GROUP, GROUP)
        cells = cell_ref[pl.ds(first, GROUP), :]
        weights = weight_ref[pl.ds(first, GROUP), :]
        for k in range(GROUP):
            cell = cells[k : k + 1]
            found = jnp.dot(
                table_ref[...],
                one_hot(cell & (LANES - 1), LANES),
                preferred_element_type=jnp.float32,
            )
            base = cell // LANES - lax.broadcasted_iota(jnp.int32, (8, slots), 0) // 4
            total = jnp.zeros((8, slots), jnp.float32)
            for j in range(rows // 8):
                value = found[8 * j : 8 * j + 8]
                for t in range(1, TERMS):
                    value = value + found[t * rows + 8 * j : t * rows + 8 * j + 8]
                total = total + jnp.where(base == 2 * j, value, 0.0)
            out_ref[first + k] = (total[0:4] + total[4:8]) * weights[k : k + 1]

    each_owner(owners, body)


def exchange_kernel(come_ref, cell_ref, top_ref, push_ref, out_ref, sum_ref, table_ref):
    owners, slots = cell_ref.shape
    rows, cols = top_ref.shape[1:]
    high = rows * cols // LANES
    sum_ref[...] = jnp.zeros_like(sum_ref)

    def add(group):
        first = pl.multiple_of(group * GROUP, GROUP)
        cells = cell_ref[pl.ds(first, GROUP), :]
        for k in range(GROUP):
            cell = cells[k : k + 1]
            col = cell % cols
            spot = (col // LANES) * rows + cell // cols
            mask = lax.broadcasted_iota(jnp.int32, (high, slots), 0) == spot
            left = []
            for term in cut(come_ref[first + k]):
                wide = term.astype(jnp.float32)
                for f in range(4):
                    left.append(jnp.where(mask, wide[f : f + 1], 0.0))
            sum_ref[...] += lax.dot_general(
                jnp.concatenate(left, 0).astype(jnp.bfloat16),
                one_hot(col % LANES, LANES),
                (((1,), (1,)), ((), ())),
                preferred_element_type=jnp.float32,
            )

    each_owner(owners, add)
    for f in range(4):
        for b in range(cols // LANES):
            span = slice(b * LANES, (b + 1) * LANES)
            value = 0.0
            for t in reversed(range(TERMS)):
                at = (t * 4 + f) * high + b * rows
                value = value + sum_ref[at : at + rows, :]
            push_ref[f, :, span] = value
            surface = top_ref[f, :, span] + value * top_ref[4, :, span]
            for t, term in enumerate(cut(surface)):
                at = (t * 4 + f) * high + b * rows
                table_ref[at : at + rows, :] = term

    def pick(group):
        first = pl.multiple_of(group * GROUP, GROUP)
        cells = cell_ref[pl.ds(first, GROUP), :]
        for k in range(GROUP):
            cell = cells[k : k + 1]
            col = cell % cols
            spot = (col // LANES) * rows + cell // cols
            found = jnp.dot(
                table_ref[...],
                one_hot(col % LANES, LANES),
                preferred_element_type=jnp.float32,
            )
            base = spot - lax.broadcasted_iota(jnp.int32, (8, slots), 0)
            masks = [base == 8 * j for j in range(high // 8)]
            picked = []
            for f in range(4):
                total = jnp.zeros((8, slots), jnp.float32)
                for j in range(high // 8):
                    at = f * high + 8 * j
                    value = found[at : at + 8]
                    for t in range(1, TERMS):
                        value = value + found[t * 4 * high + at : t * 4 * high + at + 8]
                    total = total + jnp.where(masks[j], value, 0.0)
                picked.append(jnp.sum(total, axis=0, keepdims=True))
            out_ref[first + k] = jnp.concatenate(picked, 0)

    each_owner(owners, pick)


def weight_kernel(cell_ref, weight_ref, out_ref, sum_ref):
    owners, slots = cell_ref.shape
    high = sum_ref.shape[0] // TERMS
    sum_ref[...] = jnp.zeros_like(sum_ref)

    def body(group):
        first = pl.multiple_of(group * GROUP, GROUP)
        cells = cell_ref[pl.ds(first, GROUP), :]
        weights = weight_ref[pl.ds(first, GROUP), :]
        for k in range(GROUP):
            cell = cells[k : k + 1]
            mask = lax.broadcasted_iota(jnp.int32, (high, slots), 0) == cell // LANES
            left = [
                jnp.where(mask, term.astype(jnp.float32), 0.0)
                for term in cut(weights[k : k + 1])
            ]
            sum_ref[...] += lax.dot_general(
                jnp.concatenate(left, 0).astype(jnp.bfloat16),
                one_hot(cell & (LANES - 1), LANES),
                (((1,), (1,)), ((), ())),
                preferred_element_type=jnp.float32,
            )

    each_owner(owners, body)
    value = 0.0
    for t in reversed(range(TERMS)):
        value = value + sum_ref[t * high : (t + 1) * high, :]
    out_ref[...] = 1.0 / jnp.maximum(value, 1.0)


def return_kernel(come_ref, cell_ref, weight_ref, inverse_ref, out_ref, sum_ref):
    owners, slots = cell_ref.shape
    blocks = out_ref.shape[1] // LANES
    rows = sum_ref.shape[0] // TERMS
    sum_ref[...] = jnp.zeros_like(sum_ref)

    def body(group):
        first = pl.multiple_of(group * GROUP, GROUP)
        cells = cell_ref[pl.ds(first, GROUP), :]
        weights = weight_ref[pl.ds(first, GROUP), :]
        for k in range(GROUP):
            cell = cells[k : k + 1]
            base = cell // LANES - lax.broadcasted_iota(jnp.int32, (8, slots), 0) // 4
            left = []
            for term in cut(come_ref[first + k] * weights[k : k + 1]):
                wide = term.astype(jnp.float32)
                wide = jnp.concatenate([wide, wide], 0)
                for j in range(rows // 8):
                    left.append(jnp.where(base == 2 * j, wide, 0.0))
            sum_ref[...] += lax.dot_general(
                jnp.concatenate(left, 0).astype(jnp.bfloat16),
                one_hot(cell & (LANES - 1), LANES),
                (((1,), (1,)), ((), ())),
                preferred_element_type=jnp.float32,
            )

    each_owner(owners, body)
    for block in range(blocks):
        value = 0.0
        for t in reversed(range(TERMS)):
            at = t * rows + 4 * block
            value = value + sum_ref[at : at + 4, :]
        out_ref[:, block * LANES : (block + 1) * LANES] = (
            value * inverse_ref[block : block + 1, :]
        )


def up_to(count, step):
    return (count + step - 1) // step * step


def call(kernel, out_shapes, scratch, *operands, far=0, copies=0, limit=VMEM_BYTES, flops=0):
    vmem = pl.BlockSpec(memory_space=pltpu.VMEM)
    return pl.pallas_call(
        kernel,
        out_shape=[jax.ShapeDtypeStruct(shape, jnp.float32) for shape in out_shapes],
        in_specs=[pl.BlockSpec(memory_space=pltpu.HBM)] * far + [vmem] * (len(operands) - far),
        scratch_shapes=[pltpu.VMEM(shape, dtype) for shape, dtype in scratch]
        + [pltpu.SemaphoreType.DMA((copies,))] * (copies > 0),
        compiler_params=pltpu.CompilerParams(vmem_limit_bytes=limit),
        cost_estimate=pl.CostEstimate(
            flops=flops,
            transcendentals=0,
            bytes_accessed=sum(x.size * x.dtype.itemsize for x in operands)
            + sum(4 * math.prod(shape) for shape in out_shapes),
        ),
    )(*operands)


HALO = 2
EDGE = 128


def edge_kernel(t_ref, s_ref, u_ref, v_ref, wet_ref, west_ref, east_ref, left, right, wet, sem):
    levels, rows, cols = t_ref.shape
    count = levels * rows
    copies = []
    for f, ref in enumerate((t_ref, s_ref, u_ref, v_ref)):
        copies.append(
            (
                pltpu.make_async_copy(ref.at[:, :, :EDGE], left.at[f], sem.at[2 * f]),
                pltpu.make_async_copy(ref.at[:, :, cols - EDGE :], right.at[f], sem.at[2 * f + 1]),
            )
        )
    copies.append((pltpu.make_async_copy(wet_ref, wet, sem.at[8]),))
    for group in copies:
        for copy in group:
            copy.start()

    def sides(left, right):
        side = lax.broadcasted_iota(jnp.int32, left.shape, 1) < EDGE // 2
        turned = jnp.where(side, left, right).T
        return turned[:HALO], turned[EDGE - HALO :]

    for f in range(4):
        for copy in copies[f]:
            copy.wait()
        west, east = sides(left[f].reshape(count, EDGE), right[f].reshape(count, EDGE))
        west_ref[HALO * f : HALO * f + HALO, :] = west
        east_ref[HALO * f : HALO * f + HALO, :] = east
    copies[4][0].wait()
    west, east = sides(
        wet[:, :EDGE].astype(jnp.float32), wet[:, cols - EDGE :].astype(jnp.float32)
    )
    west_ref[HALO * 4 : HALO * 5, :] = jnp.zeros((HALO, count), jnp.float32)
    east_ref[HALO * 4 : HALO * 5, :] = jnp.zeros((HALO, count), jnp.float32)
    west_ref[HALO * 4 : HALO * 5, :rows] = west
    east_ref[HALO * 4 : HALO * 5, :rows] = east


def rows_kernel(t_ref, s_ref, u_ref, v_ref, wet_ref, from_west_ref, from_east_ref,
                down_ref, up_ref, side_ref):
    levels, rows, cols = t_ref.shape

    def turned(f, count):
        return jnp.concatenate(
            [
                from_east_ref[HALO * f : HALO * f + HALO, :count],
                jnp.zeros((EDGE - 2 * HALO, count), jnp.float32),
                from_west_ref[HALO * f : HALO * f + HALO, :count],
            ],
            0,
        ).T

    for f, ref in enumerate((t_ref, s_ref, u_ref, v_ref)):
        span = slice(f * levels, (f + 1) * levels)
        side = turned(f, levels * rows).reshape(levels, rows, EDGE)
        side_ref[span] = side
        down_ref[span, :, :cols] = ref[:, :HALO, :]
        up_ref[span, :, :cols] = ref[:, rows - HALO :, :]
        down_ref[span, :, cols:] = side[:, :HALO, :]
        up_ref[span, :, cols:] = side[:, rows - HALO :, :]
    side = turned(4, rows)
    wet = wet_ref[...].astype(jnp.float32)
    side_ref[4 * levels] = side
    down_ref[4 * levels, :, :cols] = wet[:HALO]
    up_ref[4 * levels, :, :cols] = wet[rows - HALO :]
    down_ref[4 * levels, :, cols:] = side[:HALO]
    up_ref[4 * levels, :, cols:] = side[rows - HALO :]


def ocean_kernel(total_rows, t_in, s_in, u_in, v_in, wet_in, side_in, north_in, fold_in,
                 south_in, mix_in, part_out, factor_out, reply_out, top_ref,
                 t_ref, s_ref, u_ref, v_ref, wet_ref, side_ref, north_ref, fold_ref, south_ref,
                 mix_ref, part_ref, scale_ref, factor_ref, reply_ref, east_gate, north_gate,
                 turn_ref, state_ref, middle_ref, before_ref, in_sem, out_sem):
    levels, rows, cols = t_ref.shape
    tall = rows + 8
    tiles = cols // EDGE
    spans = [slice(j * EDGE, (j + 1) * EDGE) for j in range(tiles + 1)]
    stripe = lax.axis_index("ocn")
    on_top = stripe == lax.axis_size("ocn") - 1
    copies = [
        pltpu.make_async_copy(source, target, in_sem.at[i])
        for i, (source, target) in enumerate(
            (
                (mix_in, mix_ref),
                (wet_in, wet_ref),
                (north_in, north_ref),
                (south_in, south_ref),
                (fold_in, fold_ref),
                (side_in, side_ref),
                (t_in, t_ref),
                (s_in, s_ref),
                (u_in, u_ref),
                (v_in, v_ref),
            )
        )
    ]
    for copy in copies:
        copy.start()

    copies[0].wait()
    above = jnp.zeros((rows, cols), jnp.float32)
    factor = above
    reply = None
    for k in range(levels):
        below = mix_ref[k] if k < levels - 1 else jnp.zeros_like(above)
        scale = 1.0 / (1.0 + above + below + above * factor)
        factor = -below * scale
        reply = scale if k == 0 else above * reply * scale
        scale_ref[k] = scale
        factor_ref[k] = factor
        reply_ref[k] = reply
        above = below
    factor_copy = pltpu.make_async_copy(factor_ref, factor_out, out_sem.at[1])
    factor_copy.start()
    copies[1].wait()
    open_water = wet_ref[...].astype(jnp.float32)
    for k in range(levels - 2, -1, -1):
        reply_ref[k + 1] = reply * open_water
        reply = reply_ref[k] - factor_ref[k] * reply
    reply_ref[0] = reply * open_water
    top_ref[4] = reply * open_water
    reply_copy = pltpu.make_async_copy(reply_ref, reply_out, out_sem.at[2])
    reply_copy.start()
    for copy in copies[2:]:
        copy.wait()

    @pl.when(on_top)
    def _():
        flip = EDGE - 1 - lax.broadcasted_iota(jnp.int32, (8, EDGE), 1)
        order = list(range(tiles))[::-1] + [tiles]
        blank = jnp.zeros((8 - HALO, EDGE), jnp.float32)

        def mirror(channel, sign):
            fold = fold_ref[channel]
            for j, span in enumerate(spans):
                part = fold[:, spans[order[j]]]
                part = jnp.concatenate([part[1:2], part[0:1], blank], 0)
                part = jnp.take_along_axis(part, flip, axis=1)
                north_ref[channel, :, span] = part[:HALO] * sign

        def mirror_level(k, carry):
            for f in range(4):
                mirror(f * levels + k, 1.0 if f < 2 else -1.0)
            return carry

        lax.fori_loop(0, levels, mirror_level, 0)
        mirror(4 * levels, 1.0)

    gap = jnp.zeros((8 - 2 * HALO, EDGE), jnp.float32)

    def beyond(channel, span):
        return jnp.concatenate([north_ref[channel, :, span], gap, south_ref[channel, :, span]], 0)

    lane = lax.broadcasted_iota(jnp.int32, (tall, EDGE), 1)
    first = lane == 0
    final = lane == EDGE - 1
    count = tiles + 1

    def ring(ref, centre, outer):
        ref[8 : 8 + rows] = centre
        ref[8 + rows : 8 + tall] = outer
        ref[0:8] = outer
        ref[8 + tall : 16 + tall] = centre[0:8]

    def ahead(x):
        return pltpu.roll(x, EDGE - 1, 1)

    def behind(x):
        return pltpu.roll(x, 1, 1)

    row = lax.broadcasted_iota(jnp.int32, (tall, EDGE), 0)
    row = jnp.where(row >= tall - HALO, row - tall, row) + stripe * rows
    row = jnp.where(row >= total_rows, 2 * total_rows - 1 - row, row)
    latitude = jnp.pi * ((row.astype(jnp.float32) + 0.5) / total_rows - 0.5)
    turn = coriolis * jnp.sin(latitude)
    for j, span in enumerate(spans):
        ring(
            state_ref.at[0, j],
            open_water[:, span] if j < tiles else side_ref[4 * levels],
            beyond(4 * levels, span),
        )
    for j in range(count):
        wet = state_ref[0, j, 8 : 8 + tall]
        after = state_ref[0, (j + 1) % count, 8 : 8 + tall]
        east_gate[j] = wet * jnp.where(final, ahead(after), ahead(wet))
        north = wet * state_ref[0, j, 9 : 9 + tall]
        ring(north_gate.at[j], north[:rows], north[rows:])
        turn_ref[j] = turn * wet

    def substep(source, order, height, put):
        def rolled(j):
            return [ahead(source[f, j, 8 : 8 + height]) for f in range(4)]

        def eastward(j, here, after):
            gate = east_gate[j, :height]
            return [
                gate
                * (jnp.where(final[:height], after[f], here[f]) - source[f, j, 8 : 8 + height])
                for f in range(4)
            ]

        here = rolled(order[0])
        passed = [behind(x) for x in eastward(order[-1], rolled(order[-1]), here)]
        for j in order[:-1]:
            after = rolled((j + 1) % count)
            east = eastward(j, here, after)
            here = after
            before, passed = passed, [behind(x) for x in east]
            west = [jnp.where(first[:height], p, q) for p, q in zip(before, passed)]
            north_open = north_gate[j, 8 : 8 + height]
            south_open = north_gate[j, 7 : 7 + height]
            value = [source[f, j, 8 : 8 + height] for f in range(4)]
            north = [
                north_open * (source[f, j, 9 : 9 + height] - value[f]) for f in range(4)
            ]
            south = [
                south_open * (value[f] - source[f, j, 7 : 7 + height]) for f in range(4)
            ]
            cx = courant_scale * value[2]
            cy = courant_scale * value[3]
            to_east = diffusion - jnp.minimum(cx, 0.0)
            to_west = diffusion + jnp.maximum(cx, 0.0)
            to_north = diffusion - jnp.minimum(cy, 0.0)
            to_south = diffusion + jnp.maximum(cy, 0.0)
            for f in range(2):
                put(
                    f,
                    j,
                    value[f]
                    + (
                        (to_east * east[f] - to_west * west[f])
                        + (to_north * north[f] - to_south * south[f])
                    ),
                )
            turning = turn_ref[j, :height]
            for f, other in ((2, turning * value[3]), (3, -turning * value[2])):
                put(
                    f,
                    j,
                    value[f]
                    + (viscosity * ((east[f] - west[f]) + (north[f] - south[f])) + other),
                )

    def level(k, carry):
        for f, ref in enumerate((t_ref, s_ref, u_ref, v_ref)):
            channel = f * levels + k
            for j, span in enumerate(spans):
                ring(
                    state_ref.at[f, j],
                    ref[k, :, span] if j < tiles else side_ref[channel],
                    beyond(channel, span),
                )

        def put_middle(f, j, value):
            middle_ref[k, f, j, 8 : 8 + tall] = value
            middle_ref[k, f, j, 0:8] = value[rows:]

        substep(state_ref, [tiles] + list(range(tiles)) + [tiles - 1], tall, put_middle)
        return carry

    def last_level(k, carry):
        before = jnp.maximum(k - 1, 0)
        start = jnp.where(k > 0, 1.0, 0.0)

        def put_part(f, j, value):
            span = spans[j]
            above = start * mix_ref[before, :, span]
            value = (value + above * before_ref[f, :, span]) * scale_ref[k, :, span]
            before_ref[f, :, span] = value
            part_ref[k, f, :, span] = value

        substep(middle_ref.at[k], list(range(tiles)) + [tiles], rows, put_part)
        pltpu.make_async_copy(part_ref.at[k], part_out.at[k], out_sem.at[0]).start()
        return carry

    before_ref[...] = jnp.zeros_like(before_ref)
    lax.fori_loop(0, levels, level, 0)
    lax.fori_loop(0, levels, last_level, 0)

    def back(j, solved):
        k = levels - 2 - j
        factor = factor_ref[k]
        return tuple(part_ref[k, f] - factor * solved[f] for f in range(4))

    solved = lax.fori_loop(0, levels - 1, back, tuple(part_ref[levels - 1, f] for f in range(4)))
    for f in range(4):
        top_ref[f] = solved[f]
    pltpu.make_async_copy(part_ref, part_out, out_sem.at[0]).wait()
    factor_copy.wait()
    reply_copy.wait()


def finish_kernel(part_ref, factor_ref, reply_ref, push_ref, t_out, s_out, u_out, v_out):
    levels = t_out.shape[0]
    outs = (t_out, s_out, u_out, v_out)
    last = levels - 1
    for f in range(4):
        outs[f][last] = part_ref[last, f] + push_ref[f] * reply_ref[last]

    def back(j, solved):
        k = last - 1 - j
        factor = factor_ref[k]
        reply = reply_ref[k]
        solved = tuple(part_ref[k, f] - factor * solved[f] for f in range(4))
        for f in range(4):
            outs[f][k] = solved[f] + push_ref[f] * reply
        return solved

    lax.fori_loop(0, last, back, tuple(part_ref[last, f] for f in range(4)))


def per_device(
    atm_flux, send_cell, send_weight, recv_cell, temp, salt, uvel, vvel, wet_mask, vert_mix
):
    levels, block_rows, block_cols = temp.shape
    slot_cells = send_cell[0]
    slot_weights = send_weight[0]
    arrival_cells = recv_cell[0]
    owners, capacity = slot_cells.shape
    atm_cells = atm_flux.shape[1]
    blocks = atm_cells // LANES
    rows = up_to(4 * blocks, 16)
    high = block_rows * block_cols // LANES
    wide = block_cols + EDGE
    columns = lax.axis_size("atm")
    stripes = lax.axis_size("ocn")
    whole = (levels, block_rows, block_cols)
    ocean = (temp, salt, uvel, vvel)

    edge = (5 * HALO, levels * block_rows)
    strips = (4, levels, block_rows, EDGE)
    west, east = call(
        edge_kernel,
        [edge, edge],
        [
            (strips, jnp.float32),
            (strips, jnp.float32),
            ((block_rows, block_cols), jnp.int32),
        ],
        *ocean,
        wet_mask,
        far=5,
        copies=9,
    )
    from_east = lax.ppermute(west, "atm", [((i + 1) % columns, i) for i in range(columns)])
    from_west = lax.ppermute(east, "atm", [(i, (i + 1) % columns) for i in range(columns)])

    strip = (4 * levels + 1, HALO, wide)
    down, up, side = call(
        rows_kernel,
        [strip, strip, (4 * levels + 1, block_rows, EDGE)],
        [],
        *ocean,
        wet_mask,
        from_west,
        from_east,
    )
    north = lax.ppermute(down, "ocn", [(i + 1, i) for i in range(stripes - 1)])
    south = lax.ppermute(up, "ocn", [(i, i + 1) for i in range(stripes - 1)])
    last = stripes - 1
    fold = lax.ppermute(
        up,
        ("atm", "ocn"),
        [(i * stripes + last, (columns - 1 - i) * stripes + last) for i in range(columns)],
    )
    (outgoing,) = call(
        send_kernel,
        [(owners, 4, capacity)],
        [
            (atm_flux.shape, jnp.float32),
            (slot_cells.shape, jnp.int32),
            (slot_cells.shape, jnp.float32),
            ((rows, LANES), jnp.float32),
            ((TERMS * rows, LANES), jnp.bfloat16),
        ],
        atm_flux,
        slot_cells,
        slot_weights,
        far=3,
        copies=3,
        flops=2 * TERMS * rows * LANES * owners * capacity,
    )
    outgoing, north, south, fold = lax.optimization_barrier((outgoing, north, south, fold))
    incoming = lax.all_to_all(outgoing, ("atm", "ocn"), split_axis=0, concat_axis=0, tiled=True)
    (inverse,) = call(
        weight_kernel,
        [(up_to(blocks, 16), LANES)],
        [((TERMS * up_to(blocks, 16), LANES), jnp.float32)],
        slot_cells,
        slot_weights,
        limit=SMALL_BYTES,
        flops=2 * TERMS * up_to(blocks, 16) * LANES * owners * capacity,
    )
    vmem = pl.BlockSpec(memory_space=pltpu.VMEM)
    far = pl.BlockSpec(memory_space=pltpu.HBM)
    tall = block_rows + 8
    tiles = wide // EDGE
    plane = (block_rows, block_cols)
    shapes = [(levels, 4, *plane), whole, whole, (5, *plane)]
    part, factor, reply, top = pl.pallas_call(
        functools.partial(ocean_kernel, block_rows * stripes),
        out_shape=[jax.ShapeDtypeStruct(shape, jnp.float32) for shape in shapes],
        in_specs=[far] * 10,
        out_specs=[far] * 3 + [vmem],
        scratch_shapes=[
            *[pltpu.VMEM(whole, jnp.float32)] * 4,
            pltpu.VMEM(plane, jnp.int32),
            pltpu.VMEM(side.shape, jnp.float32),
            pltpu.VMEM(strip, jnp.float32),
            pltpu.VMEM(strip, jnp.float32),
            pltpu.VMEM(strip, jnp.float32),
            pltpu.VMEM(vert_mix.shape, jnp.float32),
            pltpu.VMEM(shapes[0], jnp.float32),
            pltpu.VMEM(whole, jnp.float32),
            pltpu.VMEM(whole, jnp.float32),
            pltpu.VMEM(whole, jnp.float32),
            pltpu.VMEM((tiles, tall, EDGE), jnp.float32),
            pltpu.VMEM((tiles, tall + 16, EDGE), jnp.float32),
            pltpu.VMEM((tiles, tall, EDGE), jnp.float32),
            pltpu.VMEM((4, tiles, tall + 16, EDGE), jnp.float32),
            pltpu.VMEM((levels, 4, tiles, tall + 16, EDGE), jnp.float32),
            pltpu.VMEM((4, *plane), jnp.float32),
            pltpu.SemaphoreType.DMA((10,)),
            pltpu.SemaphoreType.DMA((3,)),
        ],
        compiler_params=pltpu.CompilerParams(vmem_limit_bytes=VMEM_BYTES),
        cost_estimate=pl.CostEstimate(
            flops=80 * 4 * 2 * temp.size, transcendentals=0, bytes_accessed=4 * 13 * temp.size
        ),
    )(*ocean, wet_mask, side, north, fold, south, vert_mix)

    push, leaving = call(
        exchange_kernel,
        [(4, block_rows, block_cols), (owners, 4, capacity)],
        [
            ((TERMS * 4 * high, LANES), jnp.float32),
            ((TERMS * 4 * high, LANES), jnp.bfloat16),
        ],
        incoming,
        arrival_cells,
        top,
        limit=SMALL_BYTES,
        flops=2 * 2 * TERMS * 4 * high * LANES * owners * capacity,
    )
    returning = lax.all_to_all(leaving, ("atm", "ocn"), split_axis=0, concat_axis=0, tiled=True)
    finished = call(finish_kernel, [whole] * 4, [], part, factor, reply, push)
    (atm_surface,) = call(
        return_kernel,
        [(4, atm_cells)],
        [((TERMS * rows, LANES), jnp.float32)],
        returning,
        slot_cells,
        slot_weights,
        inverse,
        limit=SMALL_BYTES,
        flops=2 * TERMS * rows * LANES * owners * capacity,
    )
    return (*finished, atm_surface)


def solution(mesh):
    in_specs = (
        P(None, ("atm", "ocn")),
        P(("atm", "ocn"), None, None),
        P(("atm", "ocn"), None, None),
        P(("atm", "ocn"), None, None),
        P(None, "ocn", "atm"),
        P(None, "ocn", "atm"),
        P(None, "ocn", "atm"),
        P(None, "ocn", "atm"),
        P("ocn", "atm"),
        P(None, "ocn", "atm"),
    )
    out_specs = (
        P(None, "ocn", "atm"),
        P(None, "ocn", "atm"),
        P(None, "ocn", "atm"),
        P(None, "ocn", "atm"),
        P(None, ("atm", "ocn")),
    )
    return jax.shard_map(
        per_device, mesh=mesh, in_specs=in_specs, out_specs=out_specs, check_vma=False
    )
```

```python
import functools
import math

import jax
import jax.numpy as jnp
from jax import lax
from jax.experimental import pallas as pl
from jax.experimental.pallas import tpu as pltpu
from jax.sharding import PartitionSpec as P

courant_scale = 0.05
diffusion = 0.15
viscosity = 0.15
coriolis = 0.1
heat_gain = 0.25
water_gain = 0.25
stress_gain = 0.25


LANES = 256
TERMS = 2
GROUP = 8
VMEM_BYTES = 60 * 2**20
SMALL_BYTES = 24 * 2**20
SIDE_BYTES = 24 * 2**20


def cut(values):
    terms = []
    rest = values
    for term_index in range(TERMS):
        term = rest.astype(jnp.bfloat16)
        terms.append(term)
        if term_index < TERMS - 1:
            rest = rest - term.astype(jnp.float32)
    return terms


def one_hot(positions, count):
    slots = positions.shape[1]
    base = positions - lax.broadcasted_iota(jnp.int32, (8, slots), 0)
    rows = [jnp.where(base == 8 * j, 1.0, 0.0) for j in range(count // 8)]
    return jnp.concatenate(rows, 0).astype(jnp.bfloat16)


def each_owner(owners, body):
    def outer(group, carry):
        body(group)
        return carry

    lax.fori_loop(0, owners // GROUP, outer, 0)


def send_kernel(
    flux_in, cell_in, weight_in, out_ref, flux_ref, cell_ref, weight_ref, raw_ref, table_ref, sem
):
    owners, slots = cell_ref.shape
    copies = [
        pltpu.make_async_copy(flux_in, flux_ref, sem.at[0]),
        pltpu.make_async_copy(cell_in, cell_ref, sem.at[1]),
        pltpu.make_async_copy(weight_in, weight_ref, sem.at[2]),
    ]
    for copy in copies:
        copy.start()
    blocks = flux_ref.shape[1] // LANES
    raw_ref[...] = jnp.zeros_like(raw_ref)
    copies[0].wait()
    for block in range(blocks):
        x = flux_ref[:, block * LANES : (block + 1) * LANES]
        heat = heat_gain * (x[0:1] + x[1:2] + x[2:3] + x[3:4])
        water = water_gain * (x[4:5] - x[5:6])
        raw_ref[4 * block : 4 * block + 4, :] = jnp.concatenate(
            [heat, water, stress_gain * x[6:8]], 0
        )
    rows = raw_ref.shape[0]
    for term_index, term in enumerate(cut(raw_ref[...])):
        table_ref[term_index * rows : (term_index + 1) * rows, :] = term
    copies[1].wait()
    copies[2].wait()

    def body(group):
        first = pl.multiple_of(group * GROUP, GROUP)
        cells = cell_ref[pl.ds(first, GROUP), :]
        weights = weight_ref[pl.ds(first, GROUP), :]
        for k in range(GROUP):
            cell = cells[k : k + 1]
            found = jnp.dot(
                table_ref[...],
                one_hot(cell & (LANES - 1), LANES),
                preferred_element_type=jnp.float32,
            )
            base = cell // LANES - lax.broadcasted_iota(jnp.int32, (8, slots), 0) // 4
            total = jnp.zeros((8, slots), jnp.float32)
            for j in range(rows // 8):
                value = found[8 * j : 8 * j + 8]
                for t in range(1, TERMS):
                    value = value + found[t * rows + 8 * j : t * rows + 8 * j + 8]
                total = total + jnp.where(base == 2 * j, value, 0.0)
            out_ref[first + k] = (total[0:4] + total[4:8]) * weights[k : k + 1]

    each_owner(owners, body)


def exchange_kernel(come_ref, cell_ref, top_ref, push_ref, out_ref, sum_ref, table_ref):
    owners, slots = cell_ref.shape
    rows, cols = top_ref.shape[1:]
    high = rows * cols // LANES
    sum_ref[...] = jnp.zeros_like(sum_ref)

    def add(group):
        first = pl.multiple_of(group * GROUP, GROUP)
        cells = cell_ref[pl.ds(first, GROUP), :]
        for k in range(GROUP):
            cell = cells[k : k + 1]
            col = cell % cols
            spot = (col // LANES) * rows + cell // cols
            mask = lax.broadcasted_iota(jnp.int32, (high, slots), 0) == spot
            left = []
            for term in cut(come_ref[first + k]):
                wide = term.astype(jnp.float32)
                for f in range(4):
                    left.append(jnp.where(mask, wide[f : f + 1], 0.0))
            sum_ref[...] += lax.dot_general(
                jnp.concatenate(left, 0).astype(jnp.bfloat16),
                one_hot(col % LANES, LANES),
                (((1,), (1,)), ((), ())),
                preferred_element_type=jnp.float32,
            )

    each_owner(owners, add)
    for f in range(4):
        for b in range(cols // LANES):
            span = slice(b * LANES, (b + 1) * LANES)
            value = 0.0
            for t in reversed(range(TERMS)):
                at = (t * 4 + f) * high + b * rows
                value = value + sum_ref[at : at + rows, :]
            push_ref[f, :, span] = value
            surface = top_ref[f, :, span] + value * top_ref[4, :, span]
            for t, term in enumerate(cut(surface)):
                at = (t * 4 + f) * high + b * rows
                table_ref[at : at + rows, :] = term

    def pick(group):
        first = pl.multiple_of(group * GROUP, GROUP)
        cells = cell_ref[pl.ds(first, GROUP), :]
        for k in range(GROUP):
            cell = cells[k : k + 1]
            col = cell % cols
            spot = (col // LANES) * rows + cell // cols
            found = jnp.dot(
                table_ref[...],
                one_hot(col % LANES, LANES),
                preferred_element_type=jnp.float32,
            )
            base = spot - lax.broadcasted_iota(jnp.int32, (8, slots), 0)
            masks = [base == 8 * j for j in range(high // 8)]
            picked = []
            for f in range(4):
                total = jnp.zeros((8, slots), jnp.float32)
                for j in range(high // 8):
                    at = f * high + 8 * j
                    value = found[at : at + 8]
                    for t in range(1, TERMS):
                        value = value + found[t * 4 * high + at : t * 4 * high + at + 8]
                    total = total + jnp.where(masks[j], value, 0.0)
                picked.append(jnp.sum(total, axis=0, keepdims=True))
            out_ref[first + k] = jnp.concatenate(picked, 0)

    each_owner(owners, pick)


def weight_kernel(cell_ref, weight_ref, out_ref, sum_ref):
    owners, slots = cell_ref.shape
    high = sum_ref.shape[0] // TERMS
    sum_ref[...] = jnp.zeros_like(sum_ref)

    def body(group):
        first = pl.multiple_of(group * GROUP, GROUP)
        cells = cell_ref[pl.ds(first, GROUP), :]
        weights = weight_ref[pl.ds(first, GROUP), :]
        for k in range(GROUP):
            cell = cells[k : k + 1]
            mask = lax.broadcasted_iota(jnp.int32, (high, slots), 0) == cell // LANES
            left = [
                jnp.where(mask, term.astype(jnp.float32), 0.0)
                for term in cut(weights[k : k + 1])
            ]
            sum_ref[...] += lax.dot_general(
                jnp.concatenate(left, 0).astype(jnp.bfloat16),
                one_hot(cell & (LANES - 1), LANES),
                (((1,), (1,)), ((), ())),
                preferred_element_type=jnp.float32,
            )

    each_owner(owners, body)
    value = 0.0
    for t in reversed(range(TERMS)):
        value = value + sum_ref[t * high : (t + 1) * high, :]
    out_ref[...] = 1.0 / jnp.maximum(value, 1.0)


def return_kernel(come_ref, cell_ref, weight_ref, inverse_ref, out_ref, sum_ref):
    owners, slots = cell_ref.shape
    blocks = out_ref.shape[1] // LANES
    rows = sum_ref.shape[0] // TERMS
    sum_ref[...] = jnp.zeros_like(sum_ref)

    def body(group):
        first = pl.multiple_of(group * GROUP, GROUP)
        cells = cell_ref[pl.ds(first, GROUP), :]
        weights = weight_ref[pl.ds(first, GROUP), :]
        for k in range(GROUP):
            cell = cells[k : k + 1]
            base = cell // LANES - lax.broadcasted_iota(jnp.int32, (8, slots), 0) // 4
            left = []
            for term in cut(come_ref[first + k] * weights[k : k + 1]):
                wide = term.astype(jnp.float32)
                wide = jnp.concatenate([wide, wide], 0)
                for j in range(rows // 8):
                    left.append(jnp.where(base == 2 * j, wide, 0.0))
            sum_ref[...] += lax.dot_general(
                jnp.concatenate(left, 0).astype(jnp.bfloat16),
                one_hot(cell & (LANES - 1), LANES),
                (((1,), (1,)), ((), ())),
                preferred_element_type=jnp.float32,
            )

    each_owner(owners, body)
    for block in range(blocks):
        value = 0.0
        for t in reversed(range(TERMS)):
            at = t * rows + 4 * block
            value = value + sum_ref[at : at + 4, :]
        out_ref[:, block * LANES : (block + 1) * LANES] = (
            value * inverse_ref[block : block + 1, :]
        )


def up_to(count, step):
    return (count + step - 1) // step * step


def call(kernel, out_shapes, scratch, *operands, far=0, copies=0, limit=VMEM_BYTES, flops=0):
    vmem = pl.BlockSpec(memory_space=pltpu.VMEM)
    return pl.pallas_call(
        kernel,
        out_shape=[jax.ShapeDtypeStruct(shape, jnp.float32) for shape in out_shapes],
        in_specs=[pl.BlockSpec(memory_space=pltpu.HBM)] * far + [vmem] * (len(operands) - far),
        scratch_shapes=[pltpu.VMEM(shape, dtype) for shape, dtype in scratch]
        + [pltpu.SemaphoreType.DMA((copies,))] * (copies > 0),
        compiler_params=pltpu.CompilerParams(vmem_limit_bytes=limit),
        cost_estimate=pl.CostEstimate(
            flops=flops,
            transcendentals=0,
            bytes_accessed=sum(x.size * x.dtype.itemsize for x in operands)
            + sum(4 * math.prod(shape) for shape in out_shapes),
        ),
    )(*operands)


HALO = 2
EDGE = 128


def edge_kernel(t_ref, s_ref, u_ref, v_ref, wet_ref, west_ref, east_ref, left, right, wet, sem):
    levels, rows, cols = t_ref.shape
    count = levels * rows
    copies = []
    for f, ref in enumerate((t_ref, s_ref, u_ref, v_ref)):
        copies.append(
            (
                pltpu.make_async_copy(ref.at[:, :, :EDGE], left.at[f], sem.at[2 * f]),
                pltpu.make_async_copy(ref.at[:, :, cols - EDGE :], right.at[f], sem.at[2 * f + 1]),
            )
        )
    copies.append((pltpu.make_async_copy(wet_ref, wet, sem.at[8]),))
    for group in copies:
        for copy in group:
            copy.start()

    def sides(left, right):
        side = lax.broadcasted_iota(jnp.int32, left.shape, 1) < EDGE // 2
        turned = jnp.where(side, left, right).T
        return turned[:HALO], turned[EDGE - HALO :]

    for f in range(4):
        for copy in copies[f]:
            copy.wait()
        west, east = sides(left[f].reshape(count, EDGE), right[f].reshape(count, EDGE))
        west_ref[HALO * f : HALO * f + HALO, :] = west
        east_ref[HALO * f : HALO * f + HALO, :] = east
    copies[4][0].wait()
    west, east = sides(
        wet[:, :EDGE].astype(jnp.float32), wet[:, cols - EDGE :].astype(jnp.float32)
    )
    west_ref[HALO * 4 : HALO * 5, :] = jnp.zeros((HALO, count), jnp.float32)
    east_ref[HALO * 4 : HALO * 5, :] = jnp.zeros((HALO, count), jnp.float32)
    west_ref[HALO * 4 : HALO * 5, :rows] = west
    east_ref[HALO * 4 : HALO * 5, :rows] = east


def strip_kernel(t_in, s_in, u_in, v_in, wet_in, down_out, up_out,
                 field_ref, wet_ref, down_ref, up_ref, in_sem, out_sem):
    fields, levels, rows, cols = field_ref.shape
    copies = [
        pltpu.make_async_copy(source, field_ref.at[f], in_sem.at[f])
        for f, source in enumerate((t_in, s_in, u_in, v_in))
    ]
    copies.append(pltpu.make_async_copy(wet_in, wet_ref, in_sem.at[fields]))
    for copy in copies:
        copy.start()
    leaving = []
    for f in range(fields + 1):
        copies[f].wait()
        if f < fields:
            span = slice(f * levels, (f + 1) * levels)
            down_ref[span] = field_ref[f, :, :HALO, :]
            up_ref[span] = field_ref[f, :, rows - HALO :, :]
        else:
            span = slice(fields * levels, fields * levels + 1)
            wet = wet_ref[...].astype(jnp.float32)
            down_ref[fields * levels] = wet[:HALO]
            up_ref[fields * levels] = wet[rows - HALO :]
        for i, (near, far) in enumerate(((down_ref, down_out), (up_ref, up_out))):
            copy = pltpu.make_async_copy(
                near.at[span], far.at[span, :, :cols], out_sem.at[2 * f + i]
            )
            copy.start()
            leaving.append(copy)
    for copy in leaving:
        copy.wait()


def side_kernel(from_west_ref, from_east_ref, down_in, up_in, down_out, up_out, side_out,
                side_ref, low_ref, high_ref, sem):
    channels, rows, _ = side_ref.shape
    levels = (channels - 1) // 4
    cols = down_out.shape[2] - EDGE

    def turned(f, count):
        return jnp.concatenate(
            [
                from_east_ref[HALO * f : HALO * f + HALO, :count],
                jnp.zeros((EDGE - 2 * HALO, count), jnp.float32),
                from_west_ref[HALO * f : HALO * f + HALO, :count],
            ],
            0,
        ).T

    for f in range(4):
        side_ref[f * levels : (f + 1) * levels] = turned(f, levels * rows).reshape(
            levels, rows, EDGE
        )
    side_ref[4 * levels] = turned(4, rows)
    low_ref[...] = side_ref[:, :HALO, :]
    high_ref[...] = side_ref[:, rows - HALO :, :]
    copies = [
        pltpu.make_async_copy(low_ref, down_out.at[:, :, cols:], sem.at[0]),
        pltpu.make_async_copy(high_ref, up_out.at[:, :, cols:], sem.at[1]),
        pltpu.make_async_copy(side_ref, side_out, sem.at[2]),
    ]
    for copy in copies:
        copy.start()
    for copy in copies:
        copy.wait()


def ocean_kernel(total_rows, t_in, s_in, u_in, v_in, wet_in, side_in, north_in, fold_in,
                 south_in, mix_in, part_out, factor_out, reply_out, top_ref,
                 t_ref, s_ref, u_ref, v_ref, wet_ref, side_ref, north_ref, fold_ref, south_ref,
                 mix_ref, part_ref, scale_ref, factor_ref, reply_ref, east_gate, north_gate,
                 turn_ref, state_ref, middle_ref, before_ref, in_sem, out_sem):
    levels, rows, cols = t_ref.shape
    tall = rows + 8
    tiles = cols // EDGE
    spans = [slice(j * EDGE, (j + 1) * EDGE) for j in range(tiles + 1)]
    stripe = lax.axis_index("ocn")
    on_top = stripe == lax.axis_size("ocn") - 1
    copies = [
        pltpu.make_async_copy(source, target, in_sem.at[i])
        for i, (source, target) in enumerate(
            (
                (mix_in, mix_ref),
                (wet_in, wet_ref),
                (north_in, north_ref),
                (south_in, south_ref),
                (fold_in, fold_ref),
                (side_in, side_ref),
                (t_in, t_ref),
                (s_in, s_ref),
                (u_in, u_ref),
                (v_in, v_ref),
            )
        )
    ]
    for copy in copies:
        copy.start()

    copies[0].wait()
    above = jnp.zeros((rows, cols), jnp.float32)
    factor = above
    reply = None
    for k in range(levels):
        below = mix_ref[k] if k < levels - 1 else jnp.zeros_like(above)
        scale = 1.0 / (1.0 + above + below + above * factor)
        factor = -below * scale
        reply = scale if k == 0 else above * reply * scale
        scale_ref[k] = scale
        factor_ref[k] = factor
        reply_ref[k] = reply
        above = below
    factor_copy = pltpu.make_async_copy(factor_ref, factor_out, out_sem.at[1])
    factor_copy.start()
    copies[1].wait()
    open_water = wet_ref[...].astype(jnp.float32)
    for k in range(levels - 2, -1, -1):
        reply_ref[k + 1] = reply * open_water
        reply = reply_ref[k] - factor_ref[k] * reply
    reply_ref[0] = reply * open_water
    top_ref[4] = reply * open_water
    reply_copy = pltpu.make_async_copy(reply_ref, reply_out, out_sem.at[2])
    reply_copy.start()
    for copy in copies[2:]:
        copy.wait()

    @pl.when(on_top)
    def _():
        flip = EDGE - 1 - lax.broadcasted_iota(jnp.int32, (8, EDGE), 1)
        order = list(range(tiles))[::-1] + [tiles]
        blank = jnp.zeros((8 - HALO, EDGE), jnp.float32)

        def mirror(channel, sign):
            fold = fold_ref[channel]
            for j, span in enumerate(spans):
                part = fold[:, spans[order[j]]]
                part = jnp.concatenate([part[1:2], part[0:1], blank], 0)
                part = jnp.take_along_axis(part, flip, axis=1)
                north_ref[channel, :, span] = part[:HALO] * sign

        def mirror_level(k, carry):
            for f in range(4):
                mirror(f * levels + k, 1.0 if f < 2 else -1.0)
            return carry

        lax.fori_loop(0, levels, mirror_level, 0, unroll=4)
        mirror(4 * levels, 1.0)

    gap = jnp.zeros((8 - 2 * HALO, EDGE), jnp.float32)

    def beyond(channel, span):
        return jnp.concatenate([north_ref[channel, :, span], gap, south_ref[channel, :, span]], 0)

    lane = lax.broadcasted_iota(jnp.int32, (tall, EDGE), 1)
    first = lane == 0
    final = lane == EDGE - 1
    count = tiles + 1

    def ring(ref, centre, outer):
        ref[8 : 8 + rows] = centre
        ref[8 + rows : 8 + tall] = outer
        ref[0:8] = outer
        ref[8 + tall : 16 + tall] = centre[0:8]

    def ahead(x):
        return pltpu.roll(x, EDGE - 1, 1)

    def behind(x):
        return pltpu.roll(x, 1, 1)

    row = lax.broadcasted_iota(jnp.int32, (tall, EDGE), 0)
    row = jnp.where(row >= tall - HALO, row - tall, row) + stripe * rows
    row = jnp.where(row >= total_rows, 2 * total_rows - 1 - row, row)
    latitude = jnp.pi * ((row.astype(jnp.float32) + 0.5) / total_rows - 0.5)
    turn = coriolis * jnp.sin(latitude)
    for j, span in enumerate(spans):
        ring(
            state_ref.at[0, j],
            open_water[:, span] if j < tiles else side_ref[4 * levels],
            beyond(4 * levels, span),
        )
    for j in range(count):
        wet = state_ref[0, j, 8 : 8 + tall]
        after = state_ref[0, (j + 1) % count, 8 : 8 + tall]
        east_gate[j] = wet * jnp.where(final, ahead(after), ahead(wet))
        north = wet * state_ref[0, j, 9 : 9 + tall]
        ring(north_gate.at[j], north[:rows], north[rows:])
        turn_ref[j] = turn * wet

    def substep(source, order, height, put):
        def rolled(j):
            return [ahead(source[f, j, 8 : 8 + height]) for f in range(4)]

        def eastward(j, here, after):
            gate = east_gate[j, :height]
            return [
                gate
                * (jnp.where(final[:height], after[f], here[f]) - source[f, j, 8 : 8 + height])
                for f in range(4)
            ]

        here = rolled(order[0])
        passed = [behind(x) for x in eastward(order[-1], rolled(order[-1]), here)]
        for j in order[:-1]:
            after = rolled((j + 1) % count)
            east = eastward(j, here, after)
            here = after
            before, passed = passed, [behind(x) for x in east]
            west = [jnp.where(first[:height], p, q) for p, q in zip(before, passed)]
            north_open = north_gate[j, 8 : 8 + height]
            south_open = north_gate[j, 7 : 7 + height]
            value = [source[f, j, 8 : 8 + height] for f in range(4)]
            north = [
                north_open * (source[f, j, 9 : 9 + height] - value[f]) for f in range(4)
            ]
            south = [
                south_open * (value[f] - source[f, j, 7 : 7 + height]) for f in range(4)
            ]
            cx = courant_scale * value[2]
            cy = courant_scale * value[3]
            to_east = diffusion - jnp.minimum(cx, 0.0)
            to_west = diffusion + jnp.maximum(cx, 0.0)
            to_north = diffusion - jnp.minimum(cy, 0.0)
            to_south = diffusion + jnp.maximum(cy, 0.0)
            for f in range(2):
                put(
                    f,
                    j,
                    value[f]
                    + (
                        (to_east * east[f] - to_west * west[f])
                        + (to_north * north[f] - to_south * south[f])
                    ),
                )
            turning = turn_ref[j, :height]
            for f, other in ((2, turning * value[3]), (3, -turning * value[2])):
                put(
                    f,
                    j,
                    value[f]
                    + (viscosity * ((east[f] - west[f]) + (north[f] - south[f])) + other),
                )

    def level(k, carry):
        for f, ref in enumerate((t_ref, s_ref, u_ref, v_ref)):
            channel = f * levels + k
            for j, span in enumerate(spans):
                ring(
                    state_ref.at[f, j],
                    ref[k, :, span] if j < tiles else side_ref[channel],
                    beyond(channel, span),
                )

        def put_middle(f, j, value):
            middle_ref[k, f, j, 8 : 8 + tall] = value
            middle_ref[k, f, j, 0:8] = value[rows:]

        substep(state_ref, [tiles] + list(range(tiles)) + [tiles - 1], tall, put_middle)
        return carry

    def last_level(k, carry):
        before = jnp.maximum(k - 1, 0)
        start = jnp.where(k > 0, 1.0, 0.0)

        def put_part(f, j, value):
            span = spans[j]
            above = start * mix_ref[before, :, span]
            value = (value + above * before_ref[f, :, span]) * scale_ref[k, :, span]
            before_ref[f, :, span] = value
            part_ref[k, f, :, span] = value

        substep(middle_ref.at[k], list(range(tiles)) + [tiles], rows, put_part)
        pltpu.make_async_copy(part_ref.at[k], part_out.at[k], out_sem.at[0]).start()
        return carry

    before_ref[...] = jnp.zeros_like(before_ref)
    lax.fori_loop(0, levels, level, 0)
    lax.fori_loop(0, levels, last_level, 0)

    def back(j, solved):
        k = levels - 2 - j
        factor = factor_ref[k]
        return tuple(part_ref[k, f] - factor * solved[f] for f in range(4))

    solved = lax.fori_loop(0, levels - 1, back, tuple(part_ref[levels - 1, f] for f in range(4)))
    for f in range(4):
        top_ref[f] = solved[f]
    pltpu.make_async_copy(part_ref, part_out, out_sem.at[0]).wait()
    factor_copy.wait()
    reply_copy.wait()


def finish_kernel(part_ref, factor_ref, reply_ref, push_ref, t_out, s_out, u_out, v_out):
    levels = t_out.shape[0]
    outs = (t_out, s_out, u_out, v_out)
    last = levels - 1
    for f in range(4):
        outs[f][last] = part_ref[last, f] + push_ref[f] * reply_ref[last]

    def back(j, solved):
        k = last - 1 - j
        factor = factor_ref[k]
        reply = reply_ref[k]
        solved = tuple(part_ref[k, f] - factor * solved[f] for f in range(4))
        for f in range(4):
            outs[f][k] = solved[f] + push_ref[f] * reply
        return solved

    lax.fori_loop(0, last, back, tuple(part_ref[last, f] for f in range(4)))


def per_device(
    atm_flux, send_cell, send_weight, recv_cell, temp, salt, uvel, vvel, wet_mask, vert_mix
):
    levels, block_rows, block_cols = temp.shape
    slot_cells = send_cell[0]
    slot_weights = send_weight[0]
    arrival_cells = recv_cell[0]
    owners, capacity = slot_cells.shape
    atm_cells = atm_flux.shape[1]
    blocks = atm_cells // LANES
    rows = up_to(4 * blocks, 16)
    high = block_rows * block_cols // LANES
    wide = block_cols + EDGE
    columns = lax.axis_size("atm")
    stripes = lax.axis_size("ocn")
    whole = (levels, block_rows, block_cols)
    ocean = (temp, salt, uvel, vvel)

    edge = (5 * HALO, levels * block_rows)
    strips = (4, levels, block_rows, EDGE)
    west, east = call(
        edge_kernel,
        [edge, edge],
        [
            (strips, jnp.float32),
            (strips, jnp.float32),
            ((block_rows, block_cols), jnp.int32),
        ],
        *ocean,
        wet_mask,
        far=5,
        copies=9,
    )
    from_east = lax.ppermute(west, "atm", [((i + 1) % columns, i) for i in range(columns)])
    from_west = lax.ppermute(east, "atm", [(i, (i + 1) % columns) for i in range(columns)])

    strip = (4 * levels + 1, HALO, wide)
    far = pl.BlockSpec(memory_space=pltpu.HBM)
    vmem = pl.BlockSpec(memory_space=pltpu.VMEM)
    main = (4 * levels + 1, HALO, block_cols)
    down, up = pl.pallas_call(
        strip_kernel,
        out_shape=[jax.ShapeDtypeStruct(strip, jnp.float32)] * 2,
        in_specs=[far] * 5,
        out_specs=[far] * 2,
        scratch_shapes=[
            pltpu.VMEM((4, *whole), jnp.float32),
            pltpu.VMEM((block_rows, block_cols), jnp.int32),
            pltpu.VMEM(main, jnp.float32),
            pltpu.VMEM(main, jnp.float32),
            pltpu.SemaphoreType.DMA((5,)),
            pltpu.SemaphoreType.DMA((10,)),
        ],
        compiler_params=pltpu.CompilerParams(vmem_limit_bytes=VMEM_BYTES),
        cost_estimate=pl.CostEstimate(
            flops=0, transcendentals=0, bytes_accessed=4 * 6 * temp.size
        ),
    )(*ocean, wet_mask)
    side_shape = (4 * levels + 1, block_rows, EDGE)
    down, up, side = pl.pallas_call(
        side_kernel,
        out_shape=[
            jax.ShapeDtypeStruct(strip, jnp.float32),
            jax.ShapeDtypeStruct(strip, jnp.float32),
            jax.ShapeDtypeStruct(side_shape, jnp.float32),
        ],
        in_specs=[vmem] * 2 + [far] * 2,
        out_specs=[far] * 3,
        scratch_shapes=[
            pltpu.VMEM(side_shape, jnp.float32),
            pltpu.VMEM((4 * levels + 1, HALO, EDGE), jnp.float32),
            pltpu.VMEM((4 * levels + 1, HALO, EDGE), jnp.float32),
            pltpu.SemaphoreType.DMA((3,)),
        ],
        input_output_aliases={2: 0, 3: 1},
        compiler_params=pltpu.CompilerParams(vmem_limit_bytes=SIDE_BYTES),
    )(from_west, from_east, down, up)
    north = lax.ppermute(down, "ocn", [(i + 1, i) for i in range(stripes - 1)])
    south = lax.ppermute(up, "ocn", [(i, i + 1) for i in range(stripes - 1)])
    last = stripes - 1
    fold = lax.ppermute(
        up,
        ("atm", "ocn"),
        [(i * stripes + last, (columns - 1 - i) * stripes + last) for i in range(columns)],
    )
    (outgoing,) = call(
        send_kernel,
        [(owners, 4, capacity)],
        [
            (atm_flux.shape, jnp.float32),
            (slot_cells.shape, jnp.int32),
            (slot_cells.shape, jnp.float32),
            ((rows, LANES), jnp.float32),
            ((TERMS * rows, LANES), jnp.bfloat16),
        ],
        atm_flux,
        slot_cells,
        slot_weights,
        far=3,
        copies=3,
        flops=2 * TERMS * rows * LANES * owners * capacity,
    )
    outgoing, north, south, fold = lax.optimization_barrier((outgoing, north, south, fold))
    incoming = lax.all_to_all(outgoing, ("atm", "ocn"), split_axis=0, concat_axis=0, tiled=True)
    (inverse,) = call(
        weight_kernel,
        [(up_to(blocks, 16), LANES)],
        [((TERMS * up_to(blocks, 16), LANES), jnp.float32)],
        slot_cells,
        slot_weights,
        limit=SMALL_BYTES,
        flops=2 * TERMS * up_to(blocks, 16) * LANES * owners * capacity,
    )
    tall = block_rows + 8
    tiles = wide // EDGE
    plane = (block_rows, block_cols)
    shapes = [(levels, 4, *plane), whole, whole, (5, *plane)]
    part, factor, reply, top = pl.pallas_call(
        functools.partial(ocean_kernel, block_rows * stripes),
        out_shape=[jax.ShapeDtypeStruct(shape, jnp.float32) for shape in shapes],
        in_specs=[far] * 10,
        out_specs=[far] * 3 + [vmem],
        scratch_shapes=[
            *[pltpu.VMEM(whole, jnp.float32)] * 4,
            pltpu.VMEM(plane, jnp.int32),
            pltpu.VMEM(side.shape, jnp.float32),
            pltpu.VMEM(strip, jnp.float32),
            pltpu.VMEM(strip, jnp.float32),
            pltpu.VMEM(strip, jnp.float32),
            pltpu.VMEM(vert_mix.shape, jnp.float32),
            pltpu.VMEM(shapes[0], jnp.float32),
            pltpu.VMEM(whole, jnp.float32),
            pltpu.VMEM(whole, jnp.float32),
            pltpu.VMEM(whole, jnp.float32),
            pltpu.VMEM((tiles, tall, EDGE), jnp.float32),
            pltpu.VMEM((tiles, tall + 16, EDGE), jnp.float32),
            pltpu.VMEM((tiles, tall, EDGE), jnp.float32),
            pltpu.VMEM((4, tiles, tall + 16, EDGE), jnp.float32),
            pltpu.VMEM((levels, 4, tiles, tall + 16, EDGE), jnp.float32),
            pltpu.VMEM((4, *plane), jnp.float32),
            pltpu.SemaphoreType.DMA((10,)),
            pltpu.SemaphoreType.DMA((3,)),
        ],
        compiler_params=pltpu.CompilerParams(vmem_limit_bytes=VMEM_BYTES),
        cost_estimate=pl.CostEstimate(
            flops=80 * 4 * 2 * temp.size, transcendentals=0, bytes_accessed=4 * 13 * temp.size
        ),
    )(*ocean, wet_mask, side, north, fold, south, vert_mix)

    push, leaving = call(
        exchange_kernel,
        [(4, block_rows, block_cols), (owners, 4, capacity)],
        [
            ((TERMS * 4 * high, LANES), jnp.float32),
            ((TERMS * 4 * high, LANES), jnp.bfloat16),
        ],
        incoming,
        arrival_cells,
        top,
        limit=SMALL_BYTES,
        flops=2 * 2 * TERMS * 4 * high * LANES * owners * capacity,
    )
    returning = lax.all_to_all(leaving, ("atm", "ocn"), split_axis=0, concat_axis=0, tiled=True)
    finished = call(finish_kernel, [whole] * 4, [], part, factor, reply, push)
    (atm_surface,) = call(
        return_kernel,
        [(4, atm_cells)],
        [((TERMS * rows, LANES), jnp.float32)],
        returning,
        slot_cells,
        slot_weights,
        inverse,
        limit=SMALL_BYTES,
        flops=2 * TERMS * rows * LANES * owners * capacity,
    )
    return (*finished, atm_surface)


def solution(mesh):
    in_specs = (
        P(None, ("atm", "ocn")),
        P(("atm", "ocn"), None, None),
        P(("atm", "ocn"), None, None),
        P(("atm", "ocn"), None, None),
        P(None, "ocn", "atm"),
        P(None, "ocn", "atm"),
        P(None, "ocn", "atm"),
        P(None, "ocn", "atm"),
        P("ocn", "atm"),
        P(None, "ocn", "atm"),
    )
    out_specs = (
        P(None, "ocn", "atm"),
        P(None, "ocn", "atm"),
        P(None, "ocn", "atm"),
        P(None, "ocn", "atm"),
        P(None, ("atm", "ocn")),
    )
    return jax.shard_map(
        per_device, mesh=mesh, in_specs=in_specs, out_specs=out_specs, check_vma=False
    )
```

```python
import functools
import math

import jax
import jax.numpy as jnp
from jax import lax
from jax.experimental import pallas as pl
from jax.experimental.pallas import tpu as pltpu
from jax.sharding import PartitionSpec as P

courant_scale = 0.05
diffusion = 0.15
viscosity = 0.15
coriolis = 0.1
heat_gain = 0.25
water_gain = 0.25
stress_gain = 0.25


LANES = 256
TERMS = 2
GROUP = 8
VMEM_BYTES = 60 * 2**20
SMALL_BYTES = 24 * 2**20
SIDE_BYTES = 24 * 2**20


def cut(values):
    terms = []
    rest = values
    for term_index in range(TERMS):
        term = rest.astype(jnp.bfloat16)
        terms.append(term)
        if term_index < TERMS - 1:
            rest = rest - term.astype(jnp.float32)
    return terms


def one_hot(positions, count):
    slots = positions.shape[1]
    base = positions - lax.broadcasted_iota(jnp.int32, (8, slots), 0)
    rows = [jnp.where(base == 8 * j, 1.0, 0.0) for j in range(count // 8)]
    return jnp.concatenate(rows, 0).astype(jnp.bfloat16)


def each_owner(owners, body):
    def outer(group, carry):
        body(group)
        return carry

    lax.fori_loop(0, owners // GROUP, outer, 0)


def send_kernel(
    flux_in, cell_in, weight_in, out_ref, flux_ref, cell_ref, weight_ref, raw_ref, table_ref, sem
):
    owners, slots = cell_ref.shape
    copies = [
        pltpu.make_async_copy(flux_in, flux_ref, sem.at[0]),
        pltpu.make_async_copy(cell_in, cell_ref, sem.at[1]),
        pltpu.make_async_copy(weight_in, weight_ref, sem.at[2]),
    ]
    for copy in copies:
        copy.start()
    blocks = flux_ref.shape[1] // LANES
    raw_ref[...] = jnp.zeros_like(raw_ref)
    copies[0].wait()
    for block in range(blocks):
        x = flux_ref[:, block * LANES : (block + 1) * LANES]
        heat = heat_gain * (x[0:1] + x[1:2] + x[2:3] + x[3:4])
        water = water_gain * (x[4:5] - x[5:6])
        raw_ref[4 * block : 4 * block + 4, :] = jnp.concatenate(
            [heat, water, stress_gain * x[6:8]], 0
        )
    rows = raw_ref.shape[0]
    for term_index, term in enumerate(cut(raw_ref[...])):
        table_ref[term_index * rows : (term_index + 1) * rows, :] = term
    copies[1].wait()
    copies[2].wait()

    def body(group):
        first = pl.multiple_of(group * GROUP, GROUP)
        cells = cell_ref[pl.ds(first, GROUP), :]
        weights = weight_ref[pl.ds(first, GROUP), :]
        for k in range(GROUP):
            cell = cells[k : k + 1]
            found = jnp.dot(
                table_ref[...],
                one_hot(cell & (LANES - 1), LANES),
                preferred_element_type=jnp.float32,
            )
            base = cell // LANES - lax.broadcasted_iota(jnp.int32, (8, slots), 0) // 4
            total = jnp.zeros((8, slots), jnp.float32)
            for j in range(rows // 8):
                value = found[8 * j : 8 * j + 8]
                for t in range(1, TERMS):
                    value = value + found[t * rows + 8 * j : t * rows + 8 * j + 8]
                total = total + jnp.where(base == 2 * j, value, 0.0)
            out_ref[first + k] = (total[0:4] + total[4:8]) * weights[k : k + 1]

    each_owner(owners, body)


def exchange_kernel(come_ref, cell_ref, top_ref, push_ref, out_ref, sum_ref, table_ref):
    owners, slots = cell_ref.shape
    rows, cols = top_ref.shape[1:]
    high = rows * cols // LANES
    sum_ref[...] = jnp.zeros_like(sum_ref)

    def add(group):
        first = pl.multiple_of(group * GROUP, GROUP)
        cells = cell_ref[pl.ds(first, GROUP), :]
        for k in range(GROUP):
            cell = cells[k : k + 1]
            col = cell % cols
            spot = (col // LANES) * rows + cell // cols
            mask = lax.broadcasted_iota(jnp.int32, (high, slots), 0) == spot
            left = []
            for term in cut(come_ref[first + k]):
                wide = term.astype(jnp.float32)
                for f in range(4):
                    left.append(jnp.where(mask, wide[f : f + 1], 0.0))
            sum_ref[...] += lax.dot_general(
                jnp.concatenate(left, 0).astype(jnp.bfloat16),
                one_hot(col % LANES, LANES),
                (((1,), (1,)), ((), ())),
                preferred_element_type=jnp.float32,
            )

    each_owner(owners, add)
    for f in range(4):
        for b in range(cols // LANES):
            span = slice(b * LANES, (b + 1) * LANES)
            value = 0.0
            for t in reversed(range(TERMS)):
                at = (t * 4 + f) * high + b * rows
                value = value + sum_ref[at : at + rows, :]
            push_ref[f, :, span] = value
            surface = top_ref[f, :, span] + value * top_ref[4, :, span]
            for t, term in enumerate(cut(surface)):
                at = (t * 4 + f) * high + b * rows
                table_ref[at : at + rows, :] = term

    def pick(group):
        first = pl.multiple_of(group * GROUP, GROUP)
        cells = cell_ref[pl.ds(first, GROUP), :]
        for k in range(GROUP):
            cell = cells[k : k + 1]
            col = cell % cols
            spot = (col // LANES) * rows + cell // cols
            found = jnp.dot(
                table_ref[...],
                one_hot(col % LANES, LANES),
                preferred_element_type=jnp.float32,
            )
            base = spot - lax.broadcasted_iota(jnp.int32, (8, slots), 0)
            masks = [base == 8 * j for j in range(high // 8)]
            picked = []
            for f in range(4):
                total = jnp.zeros((8, slots), jnp.float32)
                for j in range(high // 8):
                    at = f * high + 8 * j
                    value = found[at : at + 8]
                    for t in range(1, TERMS):
                        value = value + found[t * 4 * high + at : t * 4 * high + at + 8]
                    total = total + jnp.where(masks[j], value, 0.0)
                picked.append(jnp.sum(total, axis=0, keepdims=True))
            out_ref[first + k] = jnp.concatenate(picked, 0)

    each_owner(owners, pick)


def weight_kernel(cell_ref, weight_ref, out_ref, sum_ref):
    owners, slots = cell_ref.shape
    high = sum_ref.shape[0] // TERMS
    sum_ref[...] = jnp.zeros_like(sum_ref)

    def body(group):
        first = pl.multiple_of(group * GROUP, GROUP)
        cells = cell_ref[pl.ds(first, GROUP), :]
        weights = weight_ref[pl.ds(first, GROUP), :]
        for k in range(GROUP):
            cell = cells[k : k + 1]
            mask = lax.broadcasted_iota(jnp.int32, (high, slots), 0) == cell // LANES
            left = [
                jnp.where(mask, term.astype(jnp.float32), 0.0)
                for term in cut(weights[k : k + 1])
            ]
            sum_ref[...] += lax.dot_general(
                jnp.concatenate(left, 0).astype(jnp.bfloat16),
                one_hot(cell & (LANES - 1), LANES),
                (((1,), (1,)), ((), ())),
                preferred_element_type=jnp.float32,
            )

    each_owner(owners, body)
    value = 0.0
    for t in reversed(range(TERMS)):
        value = value + sum_ref[t * high : (t + 1) * high, :]
    out_ref[...] = 1.0 / jnp.maximum(value, 1.0)


def return_kernel(come_ref, cell_ref, weight_ref, inverse_ref, out_ref, sum_ref):
    owners, slots = cell_ref.shape
    blocks = out_ref.shape[1] // LANES
    rows = sum_ref.shape[0] // TERMS
    sum_ref[...] = jnp.zeros_like(sum_ref)

    def body(group):
        first = pl.multiple_of(group * GROUP, GROUP)
        cells = cell_ref[pl.ds(first, GROUP), :]
        weights = weight_ref[pl.ds(first, GROUP), :]
        for k in range(GROUP):
            cell = cells[k : k + 1]
            base = cell // LANES - lax.broadcasted_iota(jnp.int32, (8, slots), 0) // 4
            left = []
            for term in cut(come_ref[first + k] * weights[k : k + 1]):
                wide = term.astype(jnp.float32)
                wide = jnp.concatenate([wide, wide], 0)
                for j in range(rows // 8):
                    left.append(jnp.where(base == 2 * j, wide, 0.0))
            sum_ref[...] += lax.dot_general(
                jnp.concatenate(left, 0).astype(jnp.bfloat16),
                one_hot(cell & (LANES - 1), LANES),
                (((1,), (1,)), ((), ())),
                preferred_element_type=jnp.float32,
            )

    each_owner(owners, body)
    for block in range(blocks):
        value = 0.0
        for t in reversed(range(TERMS)):
            at = t * rows + 4 * block
            value = value + sum_ref[at : at + 4, :]
        out_ref[:, block * LANES : (block + 1) * LANES] = (
            value * inverse_ref[block : block + 1, :]
        )


def up_to(count, step):
    return (count + step - 1) // step * step


def call(kernel, out_shapes, scratch, *operands, far=0, copies=0, limit=VMEM_BYTES, flops=0):
    vmem = pl.BlockSpec(memory_space=pltpu.VMEM)
    return pl.pallas_call(
        kernel,
        out_shape=[jax.ShapeDtypeStruct(shape, jnp.float32) for shape in out_shapes],
        in_specs=[pl.BlockSpec(memory_space=pltpu.HBM)] * far + [vmem] * (len(operands) - far),
        scratch_shapes=[pltpu.VMEM(shape, dtype) for shape, dtype in scratch]
        + [pltpu.SemaphoreType.DMA((copies,))] * (copies > 0),
        compiler_params=pltpu.CompilerParams(vmem_limit_bytes=limit),
        cost_estimate=pl.CostEstimate(
            flops=flops,
            transcendentals=0,
            bytes_accessed=sum(x.size * x.dtype.itemsize for x in operands)
            + sum(4 * math.prod(shape) for shape in out_shapes),
        ),
    )(*operands)


HALO = 2
EDGE = 128


def edge_kernel(t_ref, s_ref, u_ref, v_ref, wet_ref, west_ref, east_ref, left, right, wet, sem):
    levels, rows, cols = t_ref.shape
    count = levels * rows
    copies = []
    for f, ref in enumerate((t_ref, s_ref, u_ref, v_ref)):
        copies.append(
            (
                pltpu.make_async_copy(ref.at[:, :, :EDGE], left.at[f], sem.at[2 * f]),
                pltpu.make_async_copy(ref.at[:, :, cols - EDGE :], right.at[f], sem.at[2 * f + 1]),
            )
        )
    copies.append((pltpu.make_async_copy(wet_ref, wet, sem.at[8]),))
    for group in copies:
        for copy in group:
            copy.start()

    def sides(left, right):
        side = lax.broadcasted_iota(jnp.int32, left.shape, 1) < EDGE // 2
        turned = jnp.where(side, left, right).T
        return turned[:HALO], turned[EDGE - HALO :]

    for f in range(4):
        for copy in copies[f]:
            copy.wait()
        west, east = sides(left[f].reshape(count, EDGE), right[f].reshape(count, EDGE))
        west_ref[HALO * f : HALO * f + HALO, :] = west
        east_ref[HALO * f : HALO * f + HALO, :] = east
    copies[4][0].wait()
    west, east = sides(
        wet[:, :EDGE].astype(jnp.float32), wet[:, cols - EDGE :].astype(jnp.float32)
    )
    west_ref[HALO * 4 : HALO * 5, :] = jnp.zeros((HALO, count), jnp.float32)
    east_ref[HALO * 4 : HALO * 5, :] = jnp.zeros((HALO, count), jnp.float32)
    west_ref[HALO * 4 : HALO * 5, :rows] = west
    east_ref[HALO * 4 : HALO * 5, :rows] = east


def strip_kernel(t_in, s_in, u_in, v_in, wet_in, down_out, up_out,
                 field_ref, wet_ref, down_ref, up_ref, in_sem, out_sem):
    fields, levels, rows, cols = field_ref.shape
    copies = [
        pltpu.make_async_copy(source, field_ref.at[f], in_sem.at[f])
        for f, source in enumerate((t_in, s_in, u_in, v_in))
    ]
    copies.append(pltpu.make_async_copy(wet_in, wet_ref, in_sem.at[fields]))
    for copy in copies:
        copy.start()
    leaving = []
    for f in range(fields + 1):
        copies[f].wait()
        if f < fields:
            span = slice(f * levels, (f + 1) * levels)
            down_ref[span] = field_ref[f, :, :HALO, :]
            up_ref[span] = field_ref[f, :, rows - HALO :, :]
        else:
            span = slice(fields * levels, fields * levels + 1)
            wet = wet_ref[...].astype(jnp.float32)
            down_ref[fields * levels] = wet[:HALO]
            up_ref[fields * levels] = wet[rows - HALO :]
        for i, (near, far) in enumerate(((down_ref, down_out), (up_ref, up_out))):
            copy = pltpu.make_async_copy(
                near.at[span], far.at[span, :, :cols], out_sem.at[2 * f + i]
            )
            copy.start()
            leaving.append(copy)
    for copy in leaving:
        copy.wait()


def side_kernel(from_west_ref, from_east_ref, down_in, up_in, down_out, up_out, side_out,
                side_ref, low_ref, high_ref, sem):
    channels, rows, _ = side_ref.shape
    levels = (channels - 1) // 4
    cols = down_out.shape[2] - EDGE

    def turned(f, count):
        return jnp.concatenate(
            [
                from_east_ref[HALO * f : HALO * f + HALO, :count],
                jnp.zeros((EDGE - 2 * HALO, count), jnp.float32),
                from_west_ref[HALO * f : HALO * f + HALO, :count],
            ],
            0,
        ).T

    for f in range(4):
        side_ref[f * levels : (f + 1) * levels] = turned(f, levels * rows).reshape(
            levels, rows, EDGE
        )
    side_ref[4 * levels] = turned(4, rows)
    low_ref[...] = side_ref[:, :HALO, :]
    high_ref[...] = side_ref[:, rows - HALO :, :]
    copies = [
        pltpu.make_async_copy(low_ref, down_out.at[:, :, cols:], sem.at[0]),
        pltpu.make_async_copy(high_ref, up_out.at[:, :, cols:], sem.at[1]),
        pltpu.make_async_copy(side_ref, side_out, sem.at[2]),
    ]
    for copy in copies:
        copy.start()
    for copy in copies:
        copy.wait()


def ocean_kernel(total_rows, t_in, s_in, u_in, v_in, wet_in, side_in, north_in, fold_in,
                 south_in, mix_in, part_out, factor_out, reply_out, top_ref,
                 t_ref, s_ref, u_ref, v_ref, wet_ref, side_ref, north_ref, fold_ref, south_ref,
                 mix_ref, part_ref, scale_ref, factor_ref, reply_ref, east_gate, north_gate,
                 turn_ref, state_ref, middle_ref, keep_ref, solve_ref, before_ref, in_sem, level_sem, out_sem):
    levels, rows, cols = t_ref.shape
    tall = rows + 8
    tiles = cols // EDGE
    spans = [slice(j * EDGE, (j + 1) * EDGE) for j in range(tiles + 1)]
    stripe = lax.axis_index("ocn")
    on_top = stripe == lax.axis_size("ocn") - 1
    copies = [
        pltpu.make_async_copy(source, target, in_sem.at[i])
        for i, (source, target) in enumerate(
            (
                (mix_in, mix_ref),
                (wet_in, wet_ref),
                (north_in, north_ref),
                (south_in, south_ref),
                (side_in, side_ref),
            )
        )
    ]
    fold_copy = pltpu.make_async_copy(fold_in, fold_ref, in_sem.at[5])
    for copy in copies[:4]:
        copy.start()

    @pl.when(on_top)
    def _():
        fold_copy.start()

    copies[4].start()

    def field_copy(f, k):
        source, target = ((t_in, t_ref), (s_in, s_ref), (u_in, u_ref), (v_in, v_ref))[f]
        return pltpu.make_async_copy(source.at[k], target.at[k], level_sem.at[f, k])

    def fetch(k, carry):
        for f in range(4):
            field_copy(f, k).start()
        return carry

    lax.fori_loop(0, levels, fetch, 0)

    copies[0].wait()
    above = jnp.zeros((rows, cols), jnp.float32)
    factor = above
    reply = None
    for k in range(levels):
        below = mix_ref[k] if k < levels - 1 else jnp.zeros_like(above)
        scale = 1.0 / (1.0 + above + below + above * factor)
        factor = -below * scale
        reply = scale if k == 0 else above * reply * scale
        scale_ref[k] = scale
        factor_ref[k] = factor
        reply_ref[k] = reply
        above = below
    factor_copy = pltpu.make_async_copy(factor_ref, factor_out, out_sem.at[1])
    factor_copy.start()
    copies[1].wait()
    open_water = wet_ref[...].astype(jnp.float32)
    for k in range(levels - 2, -1, -1):
        reply_ref[k + 1] = reply * open_water
        reply = reply_ref[k] - factor_ref[k] * reply
    reply_ref[0] = reply * open_water
    top_ref[4] = reply * open_water
    reply_copy = pltpu.make_async_copy(reply_ref, reply_out, out_sem.at[2])
    reply_copy.start()
    for copy in copies[2:]:
        copy.wait()

    @pl.when(on_top)
    def _():
        fold_copy.wait()
        flip = EDGE - 1 - lax.broadcasted_iota(jnp.int32, (8, EDGE), 1)
        order = list(range(tiles))[::-1] + [tiles]
        blank = jnp.zeros((8 - HALO, EDGE), jnp.float32)

        def mirror(channel, sign):
            fold = fold_ref[channel]
            for j, span in enumerate(spans):
                part = fold[:, spans[order[j]]]
                part = jnp.concatenate([part[1:2], part[0:1], blank], 0)
                part = jnp.take_along_axis(part, flip, axis=1)
                north_ref[channel, :, span] = part[:HALO] * sign

        def mirror_level(k, carry):
            for f in range(4):
                mirror(f * levels + k, 1.0 if f < 2 else -1.0)
            return carry

        lax.fori_loop(0, levels, mirror_level, 0, unroll=4)
        mirror(4 * levels, 1.0)

    gap = jnp.zeros((8 - 2 * HALO, EDGE), jnp.float32)

    def beyond(channel, span):
        return jnp.concatenate([north_ref[channel, :, span], gap, south_ref[channel, :, span]], 0)

    lane = lax.broadcasted_iota(jnp.int32, (tall, EDGE), 1)
    first = lane == 0
    final = lane == EDGE - 1
    count = tiles + 1

    def ring(ref, centre, outer):
        ref[8 : 8 + rows] = centre
        ref[8 + rows : 8 + tall] = outer
        ref[0:8] = outer
        ref[8 + tall : 16 + tall] = centre[0:8]

    def ahead(x):
        return pltpu.roll(x, EDGE - 1, 1)

    def behind(x):
        return pltpu.roll(x, 1, 1)

    row = lax.broadcasted_iota(jnp.int32, (tall, EDGE), 0)
    row = jnp.where(row >= tall - HALO, row - tall, row) + stripe * rows
    row = jnp.where(row >= total_rows, 2 * total_rows - 1 - row, row)
    latitude = jnp.pi * ((row.astype(jnp.float32) + 0.5) / total_rows - 0.5)
    turn = coriolis * jnp.sin(latitude)
    for j, span in enumerate(spans):
        ring(
            state_ref.at[0, j],
            open_water[:, span] if j < tiles else side_ref[4 * levels],
            beyond(4 * levels, span),
        )
    for j in range(count):
        wet = state_ref[0, j, 8 : 8 + tall]
        after = state_ref[0, (j + 1) % count, 8 : 8 + tall]
        east_gate[j] = wet * jnp.where(final, ahead(after), ahead(wet))
        north = wet * state_ref[0, j, 9 : 9 + tall]
        ring(north_gate.at[j], north[:rows], north[rows:])
        turn_ref[j] = turn * wet

    def substep(source, closed, height, put):
        def rolled(j):
            return [ahead(source[f, j, 8 : 8 + height]) for f in range(4)]

        def eastward(j, here, after):
            gate = east_gate[j, :height]
            return [
                gate
                * (jnp.where(final[:height], after[f], here[f]) - source[f, j, 8 : 8 + height])
                for f in range(4)
            ]

        here = rolled(0)
        side = rolled(tiles)
        side_east = eastward(tiles, side, here)
        passed = [behind(x) for x in side_east]
        for j in range(count if closed else tiles):
            if j < tiles:
                after = rolled(j + 1) if j + 1 < tiles else side
                east = eastward(j, here, after)
            else:
                after, east = None, side_east
            here = after
            before = passed
            passed = [behind(x) for x in east]
            west = [jnp.where(first[:height], p, q) for p, q in zip(before, passed)]
            north_open = north_gate[j, 8 : 8 + height]
            south_open = north_gate[j, 7 : 7 + height]
            value = [source[f, j, 8 : 8 + height] for f in range(4)]
            north = [
                north_open * (source[f, j, 9 : 9 + height] - value[f]) for f in range(4)
            ]
            south = [
                south_open * (value[f] - source[f, j, 7 : 7 + height]) for f in range(4)
            ]
            cx = courant_scale * value[2]
            cy = courant_scale * value[3]
            to_east = diffusion - jnp.minimum(cx, 0.0)
            to_west = diffusion + jnp.maximum(cx, 0.0)
            to_north = diffusion - jnp.minimum(cy, 0.0)
            to_south = diffusion + jnp.maximum(cy, 0.0)
            for f in range(2):
                put(
                    f,
                    j,
                    value[f]
                    + (
                        (to_east * east[f] - to_west * west[f])
                        + (to_north * north[f] - to_south * south[f])
                    ),
                )
            turning = turn_ref[j, :height]
            for f, other in ((2, turning * value[3]), (3, -turning * value[2])):
                put(
                    f,
                    j,
                    value[f]
                    + (viscosity * ((east[f] - west[f]) + (north[f] - south[f])) + other),
                )

    def level(k, carry):
        for f in range(4):
            field_copy(f, k).wait()
        for f, ref in enumerate((t_ref, s_ref, u_ref, v_ref)):
            channel = f * levels + k
            parts = [
                (
                    ref[k, :, span] if j < tiles else side_ref[channel],
                    beyond(channel, span),
                )
                for j, span in enumerate(spans)
            ]
            for j in range(count):
                ring(state_ref.at[f, j], *parts[j])
        def put_middle(f, j, value):
            middle_ref[f, j, 8 : 8 + tall] = value
            middle_ref[f, j, 0:8] = value[rows:]

        substep(state_ref, True, tall, put_middle)
        for f in range(4):
            keep_ref[k, f] = middle_ref[f, :, : 8 + tall]
        return carry

    def last_level(k, carry):
        before = jnp.maximum(k - 1, 0)
        above, scale = mix_ref[before], scale_ref[k]
        for f in range(4):
            middle_ref[f, :, : 8 + tall] = keep_ref[k, f]
        solve_ref[0] = jnp.where(k > 0, 1.0, 0.0) * above
        solve_ref[1] = scale

        def put_part(f, j, value):
            span = spans[j]
            before_ref[f, :, span] = (
                value + solve_ref[0, :, span] * before_ref[f, :, span]
            ) * solve_ref[1, :, span]

        substep(middle_ref, False, rows, put_part)
        part_ref[k] = before_ref[...]
        pltpu.make_async_copy(part_ref.at[k], part_out.at[k], out_sem.at[0]).start()
        return carry

    before_ref[...] = jnp.zeros_like(before_ref)
    lax.fori_loop(0, levels, level, 0)
    lax.fori_loop(0, levels, last_level, 0)

    def back(j, solved):
        k = levels - 2 - j
        factor = factor_ref[k]
        return tuple(part_ref[k, f] - factor * solved[f] for f in range(4))

    solved = lax.fori_loop(0, levels - 1, back, tuple(part_ref[levels - 1, f] for f in range(4)))
    for f in range(4):
        top_ref[f] = solved[f]
    pltpu.make_async_copy(part_ref, part_out, out_sem.at[0]).wait()
    factor_copy.wait()
    reply_copy.wait()


def finish_kernel(part_ref, factor_ref, reply_ref, push_ref, t_out, s_out, u_out, v_out):
    levels = t_out.shape[0]
    outs = (t_out, s_out, u_out, v_out)
    last = levels - 1
    for f in range(4):
        outs[f][last] = part_ref[last, f] + push_ref[f] * reply_ref[last]

    def back(j, solved):
        k = last - 1 - j
        factor = factor_ref[k]
        reply = reply_ref[k]
        solved = tuple(part_ref[k, f] - factor * solved[f] for f in range(4))
        for f in range(4):
            outs[f][k] = solved[f] + push_ref[f] * reply
        return solved

    lax.fori_loop(0, last, back, tuple(part_ref[last, f] for f in range(4)))


def per_device(
    atm_flux, send_cell, send_weight, recv_cell, temp, salt, uvel, vvel, wet_mask, vert_mix
):
    levels, block_rows, block_cols = temp.shape
    slot_cells = send_cell[0]
    slot_weights = send_weight[0]
    arrival_cells = recv_cell[0]
    owners, capacity = slot_cells.shape
    atm_cells = atm_flux.shape[1]
    blocks = atm_cells // LANES
    rows = up_to(4 * blocks, 16)
    high = block_rows * block_cols // LANES
    wide = block_cols + EDGE
    columns = lax.axis_size("atm")
    stripes = lax.axis_size("ocn")
    whole = (levels, block_rows, block_cols)
    ocean = (temp, salt, uvel, vvel)

    edge = (5 * HALO, levels * block_rows)
    strips = (4, levels, block_rows, EDGE)
    west, east = call(
        edge_kernel,
        [edge, edge],
        [
            (strips, jnp.float32),
            (strips, jnp.float32),
            ((block_rows, block_cols), jnp.int32),
        ],
        *ocean,
        wet_mask,
        far=5,
        copies=9,
    )
    from_east = lax.ppermute(west, "atm", [((i + 1) % columns, i) for i in range(columns)])
    from_west = lax.ppermute(east, "atm", [(i, (i + 1) % columns) for i in range(columns)])

    strip = (4 * levels + 1, HALO, wide)
    far = pl.BlockSpec(memory_space=pltpu.HBM)
    vmem = pl.BlockSpec(memory_space=pltpu.VMEM)
    main = (4 * levels + 1, HALO, block_cols)
    down, up = pl.pallas_call(
        strip_kernel,
        out_shape=[jax.ShapeDtypeStruct(strip, jnp.float32)] * 2,
        in_specs=[far] * 5,
        out_specs=[far] * 2,
        scratch_shapes=[
            pltpu.VMEM((4, *whole), jnp.float32),
            pltpu.VMEM((block_rows, block_cols), jnp.int32),
            pltpu.VMEM(main, jnp.float32),
            pltpu.VMEM(main, jnp.float32),
            pltpu.SemaphoreType.DMA((5,)),
            pltpu.SemaphoreType.DMA((10,)),
        ],
        compiler_params=pltpu.CompilerParams(vmem_limit_bytes=VMEM_BYTES),
        cost_estimate=pl.CostEstimate(
            flops=0, transcendentals=0, bytes_accessed=4 * 6 * temp.size
        ),
    )(*ocean, wet_mask)
    side_shape = (4 * levels + 1, block_rows, EDGE)
    down, up, side = pl.pallas_call(
        side_kernel,
        out_shape=[
            jax.ShapeDtypeStruct(strip, jnp.float32),
            jax.ShapeDtypeStruct(strip, jnp.float32),
            jax.ShapeDtypeStruct(side_shape, jnp.float32),
        ],
        in_specs=[vmem] * 2 + [far] * 2,
        out_specs=[far] * 3,
        scratch_shapes=[
            pltpu.VMEM(side_shape, jnp.float32),
            pltpu.VMEM((4 * levels + 1, HALO, EDGE), jnp.float32),
            pltpu.VMEM((4 * levels + 1, HALO, EDGE), jnp.float32),
            pltpu.SemaphoreType.DMA((3,)),
        ],
        input_output_aliases={2: 0, 3: 1},
        compiler_params=pltpu.CompilerParams(vmem_limit_bytes=SIDE_BYTES),
    )(from_west, from_east, down, up)
    north = lax.ppermute(down, "ocn", [(i + 1, i) for i in range(stripes - 1)])
    south = lax.ppermute(up, "ocn", [(i, i + 1) for i in range(stripes - 1)])
    last = stripes - 1
    fold = lax.ppermute(
        up,
        ("atm", "ocn"),
        [(i * stripes + last, (columns - 1 - i) * stripes + last) for i in range(columns)],
    )
    (outgoing,) = call(
        send_kernel,
        [(owners, 4, capacity)],
        [
            (atm_flux.shape, jnp.float32),
            (slot_cells.shape, jnp.int32),
            (slot_cells.shape, jnp.float32),
            ((rows, LANES), jnp.float32),
            ((TERMS * rows, LANES), jnp.bfloat16),
        ],
        atm_flux,
        slot_cells,
        slot_weights,
        far=3,
        copies=3,
        flops=2 * TERMS * rows * LANES * owners * capacity,
    )
    outgoing, north, south, fold = lax.optimization_barrier((outgoing, north, south, fold))
    incoming = lax.all_to_all(outgoing, ("atm", "ocn"), split_axis=0, concat_axis=0, tiled=True)
    (inverse,) = call(
        weight_kernel,
        [(up_to(blocks, 16), LANES)],
        [((TERMS * up_to(blocks, 16), LANES), jnp.float32)],
        slot_cells,
        slot_weights,
        limit=SMALL_BYTES,
        flops=2 * TERMS * up_to(blocks, 16) * LANES * owners * capacity,
    )
    tall = block_rows + 8
    tiles = wide // EDGE
    plane = (block_rows, block_cols)
    shapes = [(levels, 4, *plane), whole, whole, (5, *plane)]
    part, factor, reply, top = pl.pallas_call(
        functools.partial(ocean_kernel, block_rows * stripes),
        out_shape=[jax.ShapeDtypeStruct(shape, jnp.float32) for shape in shapes],
        in_specs=[far] * 10,
        out_specs=[far] * 3 + [vmem],
        scratch_shapes=[
            *[pltpu.VMEM(whole, jnp.float32)] * 4,
            pltpu.VMEM(plane, jnp.int32),
            pltpu.VMEM(side.shape, jnp.float32),
            pltpu.VMEM(strip, jnp.float32),
            pltpu.VMEM(strip, jnp.float32),
            pltpu.VMEM(strip, jnp.float32),
            pltpu.VMEM(vert_mix.shape, jnp.float32),
            pltpu.VMEM(shapes[0], jnp.float32),
            pltpu.VMEM(whole, jnp.float32),
            pltpu.VMEM(whole, jnp.float32),
            pltpu.VMEM(whole, jnp.float32),
            pltpu.VMEM((tiles, tall, EDGE), jnp.float32),
            pltpu.VMEM((tiles, tall + 16, EDGE), jnp.float32),
            pltpu.VMEM((tiles, tall, EDGE), jnp.float32),
            pltpu.VMEM((4, tiles, tall + 16, EDGE), jnp.float32),
            pltpu.VMEM((4, tiles, tall + 16, EDGE), jnp.float32),
            pltpu.VMEM((levels, 4, tiles, tall + 8, EDGE), jnp.float32),
            pltpu.VMEM((2, *plane), jnp.float32),
            pltpu.VMEM((4, *plane), jnp.float32),
            pltpu.SemaphoreType.DMA((6,)),
            pltpu.SemaphoreType.DMA((4, levels)),
            pltpu.SemaphoreType.DMA((3,)),
        ],
        compiler_params=pltpu.CompilerParams(vmem_limit_bytes=VMEM_BYTES),
        cost_estimate=pl.CostEstimate(
            flops=80 * 4 * 2 * temp.size, transcendentals=0, bytes_accessed=4 * 13 * temp.size
        ),
    )(*ocean, wet_mask, side, north, fold, south, vert_mix)

    push, leaving = call(
        exchange_kernel,
        [(4, block_rows, block_cols), (owners, 4, capacity)],
        [
            ((TERMS * 4 * high, LANES), jnp.float32),
            ((TERMS * 4 * high, LANES), jnp.bfloat16),
        ],
        incoming,
        arrival_cells,
        top,
        limit=SMALL_BYTES,
        flops=2 * 2 * TERMS * 4 * high * LANES * owners * capacity,
    )
    returning = lax.all_to_all(leaving, ("atm", "ocn"), split_axis=0, concat_axis=0, tiled=True)
    finished = call(finish_kernel, [whole] * 4, [], part, factor, reply, push)
    (atm_surface,) = call(
        return_kernel,
        [(4, atm_cells)],
        [((TERMS * rows, LANES), jnp.float32)],
        returning,
        slot_cells,
        slot_weights,
        inverse,
        limit=SMALL_BYTES,
        flops=2 * TERMS * rows * LANES * owners * capacity,
    )
    return (*finished, atm_surface)


def solution(mesh):
    in_specs = (
        P(None, ("atm", "ocn")),
        P(("atm", "ocn"), None, None),
        P(("atm", "ocn"), None, None),
        P(("atm", "ocn"), None, None),
        P(None, "ocn", "atm"),
        P(None, "ocn", "atm"),
        P(None, "ocn", "atm"),
        P(None, "ocn", "atm"),
        P("ocn", "atm"),
        P(None, "ocn", "atm"),
    )
    out_specs = (
        P(None, "ocn", "atm"),
        P(None, "ocn", "atm"),
        P(None, "ocn", "atm"),
        P(None, "ocn", "atm"),
        P(None, ("atm", "ocn")),
    )
    return jax.shard_map(
        per_device, mesh=mesh, in_specs=in_specs, out_specs=out_specs, check_vma=False
    )
```

```python
import functools
import math

import jax
import jax.numpy as jnp
from jax import lax
from jax.experimental import pallas as pl
from jax.experimental.pallas import tpu as pltpu
from jax.sharding import PartitionSpec as P

courant_scale = 0.05
diffusion = 0.15
viscosity = 0.15
coriolis = 0.1
heat_gain = 0.25
water_gain = 0.25
stress_gain = 0.25


LANES = 256
TERMS = 2
GROUP = 8
VMEM_BYTES = 60 * 2**20
SMALL_BYTES = 24 * 2**20
SIDE_BYTES = 24 * 2**20


def cut(values):
    terms = []
    rest = values
    for term_index in range(TERMS):
        term = rest.astype(jnp.bfloat16)
        terms.append(term)
        if term_index < TERMS - 1:
            rest = rest - term.astype(jnp.float32)
    return terms


def one_hot(positions, count):
    slots = positions.shape[1]
    base = positions - lax.broadcasted_iota(jnp.int32, (8, slots), 0)
    rows = [jnp.where(base == 8 * j, 1.0, 0.0) for j in range(count // 8)]
    return jnp.concatenate(rows, 0).astype(jnp.bfloat16)


def each_owner(owners, body):
    def outer(group, carry):
        body(group)
        return carry

    lax.fori_loop(0, owners // GROUP, outer, 0)


def send_kernel(
    flux_in, cell_in, weight_in, out_ref, flux_ref, cell_ref, weight_ref, raw_ref, table_ref, sem
):
    owners, slots = cell_ref.shape
    copies = [
        pltpu.make_async_copy(flux_in, flux_ref, sem.at[0]),
        pltpu.make_async_copy(cell_in, cell_ref, sem.at[1]),
        pltpu.make_async_copy(weight_in, weight_ref, sem.at[2]),
    ]
    for copy in copies:
        copy.start()
    blocks = flux_ref.shape[1] // LANES
    raw_ref[...] = jnp.zeros_like(raw_ref)
    copies[0].wait()
    for block in range(blocks):
        x = flux_ref[:, block * LANES : (block + 1) * LANES]
        heat = heat_gain * (x[0:1] + x[1:2] + x[2:3] + x[3:4])
        water = water_gain * (x[4:5] - x[5:6])
        raw_ref[4 * block : 4 * block + 4, :] = jnp.concatenate(
            [heat, water, stress_gain * x[6:8]], 0
        )
    rows = raw_ref.shape[0]
    for term_index, term in enumerate(cut(raw_ref[...])):
        table_ref[term_index * rows : (term_index + 1) * rows, :] = term
    copies[1].wait()
    copies[2].wait()

    def body(group):
        first = pl.multiple_of(group * GROUP, GROUP)
        cells = cell_ref[pl.ds(first, GROUP), :]
        weights = weight_ref[pl.ds(first, GROUP), :]
        for k in range(GROUP):
            cell = cells[k : k + 1]
            found = jnp.dot(
                table_ref[...],
                one_hot(cell & (LANES - 1), LANES),
                preferred_element_type=jnp.float32,
            )
            base = cell // LANES - lax.broadcasted_iota(jnp.int32, (8, slots), 0) // 4
            total = jnp.zeros((8, slots), jnp.float32)
            for j in range(rows // 8):
                value = found[8 * j : 8 * j + 8]
                for t in range(1, TERMS):
                    value = value + found[t * rows + 8 * j : t * rows + 8 * j + 8]
                total = total + jnp.where(base == 2 * j, value, 0.0)
            out_ref[first + k] = (total[0:4] + total[4:8]) * weights[k : k + 1]

    each_owner(owners, body)


def exchange_kernel(come_ref, cell_ref, top_ref, push_ref, out_ref, sum_ref, table_ref):
    owners, slots = cell_ref.shape
    rows, cols = top_ref.shape[1:]
    high = rows * cols // LANES
    sum_ref[...] = jnp.zeros_like(sum_ref)

    def add(group):
        first = pl.multiple_of(group * GROUP, GROUP)
        cells = cell_ref[pl.ds(first, GROUP), :]
        for k in range(GROUP):
            cell = cells[k : k + 1]
            col = cell % cols
            spot = (col // LANES) * rows + cell // cols
            mask = lax.broadcasted_iota(jnp.int32, (high, slots), 0) == spot
            left = []
            for term in cut(come_ref[first + k]):
                wide = term.astype(jnp.float32)
                for f in range(4):
                    left.append(jnp.where(mask, wide[f : f + 1], 0.0))
            sum_ref[...] += lax.dot_general(
                jnp.concatenate(left, 0).astype(jnp.bfloat16),
                one_hot(col % LANES, LANES),
                (((1,), (1,)), ((), ())),
                preferred_element_type=jnp.float32,
            )

    each_owner(owners, add)
    for f in range(4):
        for b in range(cols // LANES):
            span = slice(b * LANES, (b + 1) * LANES)
            value = 0.0
            for t in reversed(range(TERMS)):
                at = (t * 4 + f) * high + b * rows
                value = value + sum_ref[at : at + rows, :]
            push_ref[f, :, span] = value
            surface = top_ref[f, :, span] + value * top_ref[4, :, span]
            for t, term in enumerate(cut(surface)):
                at = (t * 4 + f) * high + b * rows
                table_ref[at : at + rows, :] = term

    def pick(group):
        first = pl.multiple_of(group * GROUP, GROUP)
        cells = cell_ref[pl.ds(first, GROUP), :]
        for k in range(GROUP):
            cell = cells[k : k + 1]
            col = cell % cols
            spot = (col // LANES) * rows + cell // cols
            found = jnp.dot(
                table_ref[...],
                one_hot(col % LANES, LANES),
                preferred_element_type=jnp.float32,
            )
            base = spot - lax.broadcasted_iota(jnp.int32, (8, slots), 0)
            masks = [base == 8 * j for j in range(high // 8)]
            picked = []
            for f in range(4):
                total = jnp.zeros((8, slots), jnp.float32)
                for j in range(high // 8):
                    at = f * high + 8 * j
                    value = found[at : at + 8]
                    for t in range(1, TERMS):
                        value = value + found[t * 4 * high + at : t * 4 * high + at + 8]
                    total = total + jnp.where(masks[j], value, 0.0)
                picked.append(jnp.sum(total, axis=0, keepdims=True))
            out_ref[first + k] = jnp.concatenate(picked, 0)

    each_owner(owners, pick)


def weight_kernel(cell_ref, weight_ref, out_ref, sum_ref):
    owners, slots = cell_ref.shape
    high = sum_ref.shape[0] // TERMS
    sum_ref[...] = jnp.zeros_like(sum_ref)

    def body(group):
        first = pl.multiple_of(group * GROUP, GROUP)
        cells = cell_ref[pl.ds(first, GROUP), :]
        weights = weight_ref[pl.ds(first, GROUP), :]
        for k in range(GROUP):
            cell = cells[k : k + 1]
            mask = lax.broadcasted_iota(jnp.int32, (high, slots), 0) == cell // LANES
            left = [
                jnp.where(mask, term.astype(jnp.float32), 0.0)
                for term in cut(weights[k : k + 1])
            ]
            sum_ref[...] += lax.dot_general(
                jnp.concatenate(left, 0).astype(jnp.bfloat16),
                one_hot(cell & (LANES - 1), LANES),
                (((1,), (1,)), ((), ())),
                preferred_element_type=jnp.float32,
            )

    each_owner(owners, body)
    value = 0.0
    for t in reversed(range(TERMS)):
        value = value + sum_ref[t * high : (t + 1) * high, :]
    out_ref[...] = 1.0 / jnp.maximum(value, 1.0)


def return_kernel(come_ref, cell_ref, weight_ref, inverse_ref, out_ref, sum_ref):
    owners, slots = cell_ref.shape
    blocks = out_ref.shape[1] // LANES
    rows = sum_ref.shape[0] // TERMS
    sum_ref[...] = jnp.zeros_like(sum_ref)

    def body(group):
        first = pl.multiple_of(group * GROUP, GROUP)
        cells = cell_ref[pl.ds(first, GROUP), :]
        weights = weight_ref[pl.ds(first, GROUP), :]
        for k in range(GROUP):
            cell = cells[k : k + 1]
            base = cell // LANES - lax.broadcasted_iota(jnp.int32, (8, slots), 0) // 4
            left = []
            for term in cut(come_ref[first + k] * weights[k : k + 1]):
                wide = term.astype(jnp.float32)
                wide = jnp.concatenate([wide, wide], 0)
                for j in range(rows // 8):
                    left.append(jnp.where(base == 2 * j, wide, 0.0))
            sum_ref[...] += lax.dot_general(
                jnp.concatenate(left, 0).astype(jnp.bfloat16),
                one_hot(cell & (LANES - 1), LANES),
                (((1,), (1,)), ((), ())),
                preferred_element_type=jnp.float32,
            )

    each_owner(owners, body)
    for block in range(blocks):
        value = 0.0
        for t in reversed(range(TERMS)):
            at = t * rows + 4 * block
            value = value + sum_ref[at : at + 4, :]
        out_ref[:, block * LANES : (block + 1) * LANES] = (
            value * inverse_ref[block : block + 1, :]
        )


def up_to(count, step):
    return (count + step - 1) // step * step


def call(kernel, out_shapes, scratch, *operands, far=0, copies=0, limit=VMEM_BYTES, flops=0):
    vmem = pl.BlockSpec(memory_space=pltpu.VMEM)
    return pl.pallas_call(
        kernel,
        out_shape=[jax.ShapeDtypeStruct(shape, jnp.float32) for shape in out_shapes],
        in_specs=[pl.BlockSpec(memory_space=pltpu.HBM)] * far + [vmem] * (len(operands) - far),
        scratch_shapes=[pltpu.VMEM(shape, dtype) for shape, dtype in scratch]
        + [pltpu.SemaphoreType.DMA((copies,))] * (copies > 0),
        compiler_params=pltpu.CompilerParams(vmem_limit_bytes=limit),
        cost_estimate=pl.CostEstimate(
            flops=flops,
            transcendentals=0,
            bytes_accessed=sum(x.size * x.dtype.itemsize for x in operands)
            + sum(4 * math.prod(shape) for shape in out_shapes),
        ),
    )(*operands)


HALO = 2
EDGE = 128


def edge_kernel(t_ref, s_ref, u_ref, v_ref, wet_ref, west_ref, east_ref, left, right, wet, sem):
    levels, rows, cols = t_ref.shape
    count = levels * rows
    copies = []
    for f, ref in enumerate((t_ref, s_ref, u_ref, v_ref)):
        copies.append(
            (
                pltpu.make_async_copy(ref.at[:, :, :EDGE], left.at[f], sem.at[2 * f]),
                pltpu.make_async_copy(ref.at[:, :, cols - EDGE :], right.at[f], sem.at[2 * f + 1]),
            )
        )
    copies.append((pltpu.make_async_copy(wet_ref, wet, sem.at[8]),))
    for group in copies:
        for copy in group:
            copy.start()

    def sides(left, right):
        side = lax.broadcasted_iota(jnp.int32, left.shape, 1) < EDGE // 2
        turned = jnp.where(side, left, right).T
        return turned[:HALO], turned[EDGE - HALO :]

    for f in range(4):
        for copy in copies[f]:
            copy.wait()
        west, east = sides(left[f].reshape(count, EDGE), right[f].reshape(count, EDGE))
        west_ref[HALO * f : HALO * f + HALO, :] = west
        east_ref[HALO * f : HALO * f + HALO, :] = east
    copies[4][0].wait()
    west, east = sides(
        wet[:, :EDGE].astype(jnp.float32), wet[:, cols - EDGE :].astype(jnp.float32)
    )
    west_ref[HALO * 4 : HALO * 5, :] = jnp.zeros((HALO, count), jnp.float32)
    east_ref[HALO * 4 : HALO * 5, :] = jnp.zeros((HALO, count), jnp.float32)
    west_ref[HALO * 4 : HALO * 5, :rows] = west
    east_ref[HALO * 4 : HALO * 5, :rows] = east


def send_strips(even, leaving, act):
    def go(swapped):
        for i, (up, down, out, sem) in enumerate(leaving):
            act(pltpu.make_async_copy(up if i % 2 == swapped else down, out, sem))

    @pl.when(even)
    def _():
        go(0)

    @pl.when(jnp.logical_not(even))
    def _():
        go(1)


def strip_kernel(t_in, s_in, u_in, v_in, wet_in, pair_out, next_out,
                 field_ref, wet_ref, down_ref, up_ref, in_sem, out_sem):
    fields, levels, rows, cols = field_ref.shape
    copies = [
        pltpu.make_async_copy(source, field_ref.at[f], in_sem.at[f])
        for f, source in enumerate((t_in, s_in, u_in, v_in))
    ]
    copies.append(pltpu.make_async_copy(wet_in, wet_ref, in_sem.at[fields]))
    for copy in copies:
        copy.start()
    even = lax.axis_index("ocn") % 2 == 0
    leaving = []
    for f in range(fields + 1):
        copies[f].wait()
        if f < fields:
            span = slice(f * levels, (f + 1) * levels)
            down_ref[span] = field_ref[f, :, :HALO, :]
            up_ref[span] = field_ref[f, :, rows - HALO :, :]
        else:
            span = slice(fields * levels, fields * levels + 1)
            wet = wet_ref[...].astype(jnp.float32)
            down_ref[fields * levels] = wet[:HALO]
            up_ref[fields * levels] = wet[rows - HALO :]
        leaving += [
            (up_ref.at[span], down_ref.at[span], out.at[span, :, :cols], out_sem.at[2 * f + i])
            for i, out in enumerate((pair_out, next_out))
        ]
        send_strips(even, leaving[-2:], lambda copy: copy.start())
    send_strips(even, leaving, lambda copy: copy.wait())


def side_kernel(from_west_ref, from_east_ref, pair_in, next_in, pair_out, next_out, side_out,
                side_ref, low_ref, high_ref, sem):
    channels, rows, _ = side_ref.shape
    levels = (channels - 1) // 4
    cols = pair_out.shape[2] - EDGE

    def turned(f, count):
        return jnp.concatenate(
            [
                from_east_ref[HALO * f : HALO * f + HALO, :count],
                jnp.zeros((EDGE - 2 * HALO, count), jnp.float32),
                from_west_ref[HALO * f : HALO * f + HALO, :count],
            ],
            0,
        ).T

    for f in range(4):
        side_ref[f * levels : (f + 1) * levels] = turned(f, levels * rows).reshape(
            levels, rows, EDGE
        )
    side_ref[4 * levels] = turned(4, rows)
    low_ref[...] = side_ref[:, :HALO, :]
    high_ref[...] = side_ref[:, rows - HALO :, :]
    even = lax.axis_index("ocn") % 2 == 0
    leaving = [
        (high_ref, low_ref, out.at[:, :, cols:], sem.at[i])
        for i, out in enumerate((pair_out, next_out))
    ]
    side_copy = pltpu.make_async_copy(side_ref, side_out, sem.at[2])
    side_copy.start()
    send_strips(even, leaving, lambda copy: copy.start())
    side_copy.wait()
    send_strips(even, leaving, lambda copy: copy.wait())


def ocean_kernel(total_rows, t_in, s_in, u_in, v_in, wet_in, side_in, pair_in, fold_in,
                 next_in, mix_in, part_out, factor_out, reply_out, top_ref,
                 t_ref, s_ref, u_ref, v_ref, wet_ref, side_ref, north_ref, fold_ref, south_ref,
                 mix_ref, part_ref, scale_ref, factor_ref, reply_ref, east_gate, north_gate,
                 turn_ref, state_ref, middle_ref, keep_ref, solve_ref, before_ref, in_sem, level_sem, out_sem):
    levels, rows, cols = t_ref.shape
    tall = rows + 8
    tiles = cols // EDGE
    spans = [slice(j * EDGE, (j + 1) * EDGE) for j in range(tiles + 1)]
    stripe = lax.axis_index("ocn")
    on_top = stripe == lax.axis_size("ocn") - 1
    copies = [
        pltpu.make_async_copy(source, target, in_sem.at[i])
        for i, (source, target) in enumerate(
            (
                (mix_in, mix_ref),
                (wet_in, wet_ref),
                (side_in, side_ref),
            )
        )
    ]
    fold_copy = pltpu.make_async_copy(fold_in, fold_ref, in_sem.at[5])
    even = stripe % 2 == 0
    strips = [
        (north_ref, south_ref, source, in_sem.at[3 + i])
        for i, source in enumerate((pair_in, next_in))
    ]

    def take_strips(swapped, act):
        for i, (north, south, source, sem) in enumerate(strips):
            act(pltpu.make_async_copy(source, north if i == swapped else south, sem))

    for copy in copies[:2]:
        copy.start()

    @pl.when(even)
    def _():
        take_strips(0, lambda copy: copy.start())

    @pl.when(jnp.logical_not(even))
    def _():
        take_strips(1, lambda copy: copy.start())

    @pl.when(on_top)
    def _():
        fold_copy.start()

    copies[2].start()

    def field_copy(f, k):
        source, target = ((t_in, t_ref), (s_in, s_ref), (u_in, u_ref), (v_in, v_ref))[f]
        return pltpu.make_async_copy(source.at[k], target.at[k], level_sem.at[f, k])

    def fetch(k, carry):
        for f in range(4):
            field_copy(f, k).start()
        return carry

    lax.fori_loop(0, levels, fetch, 0)

    copies[0].wait()
    above = jnp.zeros((rows, cols), jnp.float32)
    factor = above
    reply = None
    for k in range(levels):
        below = mix_ref[k] if k < levels - 1 else jnp.zeros_like(above)
        scale = 1.0 / (1.0 + above + below + above * factor)
        factor = -below * scale
        reply = scale if k == 0 else above * reply * scale
        scale_ref[k] = scale
        factor_ref[k] = factor
        reply_ref[k] = reply
        above = below
    factor_copy = pltpu.make_async_copy(factor_ref, factor_out, out_sem.at[1])
    factor_copy.start()
    copies[1].wait()
    open_water = wet_ref[...].astype(jnp.float32)
    for k in range(levels - 2, -1, -1):
        reply_ref[k + 1] = reply * open_water
        reply = reply_ref[k] - factor_ref[k] * reply
    reply_ref[0] = reply * open_water
    top_ref[4] = reply * open_water
    reply_copy = pltpu.make_async_copy(reply_ref, reply_out, out_sem.at[2])
    reply_copy.start()
    for copy in copies[2:]:
        copy.wait()

    @pl.when(even)
    def _():
        take_strips(0, lambda copy: copy.wait())

    @pl.when(jnp.logical_not(even))
    def _():
        take_strips(1, lambda copy: copy.wait())

    @pl.when(on_top)
    def _():
        fold_copy.wait()
        flip = EDGE - 1 - lax.broadcasted_iota(jnp.int32, (8, EDGE), 1)
        order = list(range(tiles))[::-1] + [tiles]
        blank = jnp.zeros((8 - HALO, EDGE), jnp.float32)

        def mirror(channel, sign):
            fold = fold_ref[channel]
            for j, span in enumerate(spans):
                part = fold[:, spans[order[j]]]
                part = jnp.concatenate([part[1:2], part[0:1], blank], 0)
                part = jnp.take_along_axis(part, flip, axis=1)
                north_ref[channel, :, span] = part[:HALO] * sign

        def mirror_level(k, carry):
            for f in range(4):
                mirror(f * levels + k, 1.0 if f < 2 else -1.0)
            return carry

        lax.fori_loop(0, levels, mirror_level, 0, unroll=4)
        mirror(4 * levels, 1.0)

    gap = jnp.zeros((8 - 2 * HALO, EDGE), jnp.float32)

    def beyond(channel, span):
        return jnp.concatenate([north_ref[channel, :, span], gap, south_ref[channel, :, span]], 0)

    lane = lax.broadcasted_iota(jnp.int32, (tall, EDGE), 1)
    first = lane == 0
    final = lane == EDGE - 1
    count = tiles + 1

    def ring(ref, centre, outer):
        ref[8 : 8 + rows] = centre
        ref[8 + rows : 8 + tall] = outer
        ref[0:8] = outer
        ref[8 + tall : 16 + tall] = centre[0:8]

    def ahead(x):
        return pltpu.roll(x, EDGE - 1, 1)

    def behind(x):
        return pltpu.roll(x, 1, 1)

    row = lax.broadcasted_iota(jnp.int32, (tall, EDGE), 0)
    row = jnp.where(row >= tall - HALO, row - tall, row) + stripe * rows
    row = jnp.where(row >= total_rows, 2 * total_rows - 1 - row, row)
    latitude = jnp.pi * ((row.astype(jnp.float32) + 0.5) / total_rows - 0.5)
    turn = coriolis * jnp.sin(latitude)
    for j, span in enumerate(spans):
        ring(
            state_ref.at[0, j],
            open_water[:, span] if j < tiles else side_ref[4 * levels],
            beyond(4 * levels, span),
        )
    for j in range(count):
        wet = state_ref[0, j, 8 : 8 + tall]
        after = state_ref[0, (j + 1) % count, 8 : 8 + tall]
        east_gate[j] = wet * jnp.where(final, ahead(after), ahead(wet))
        north = wet * state_ref[0, j, 9 : 9 + tall]
        ring(north_gate.at[j], north[:rows], north[rows:])
        turn_ref[j] = turn * wet

    def substep(source, closed, height, put):
        def rolled(j):
            return [ahead(source[f, j, 8 : 8 + height]) for f in range(4)]

        def eastward(j, here, after):
            gate = east_gate[j, :height]
            return [
                gate
                * (jnp.where(final[:height], after[f], here[f]) - source[f, j, 8 : 8 + height])
                for f in range(4)
            ]

        here = rolled(0)
        side = rolled(tiles)
        side_east = eastward(tiles, side, here)
        passed = [behind(x) for x in side_east]
        for j in range(count if closed else tiles):
            if j < tiles:
                after = rolled(j + 1) if j + 1 < tiles else side
                east = eastward(j, here, after)
            else:
                after, east = None, side_east
            here = after
            before = passed
            passed = [behind(x) for x in east]
            west = [jnp.where(first[:height], p, q) for p, q in zip(before, passed)]
            north_open = north_gate[j, 8 : 8 + height]
            south_open = north_gate[j, 7 : 7 + height]
            value = [source[f, j, 8 : 8 + height] for f in range(4)]
            north = [
                north_open * (source[f, j, 9 : 9 + height] - value[f]) for f in range(4)
            ]
            south = [
                south_open * (value[f] - source[f, j, 7 : 7 + height]) for f in range(4)
            ]
            cx = courant_scale * value[2]
            cy = courant_scale * value[3]
            to_east = diffusion - jnp.minimum(cx, 0.0)
            to_west = diffusion + jnp.maximum(cx, 0.0)
            to_north = diffusion - jnp.minimum(cy, 0.0)
            to_south = diffusion + jnp.maximum(cy, 0.0)
            for f in range(2):
                put(
                    f,
                    j,
                    value[f]
                    + (
                        (to_east * east[f] - to_west * west[f])
                        + (to_north * north[f] - to_south * south[f])
                    ),
                )
            turning = turn_ref[j, :height]
            for f, other in ((2, turning * value[3]), (3, -turning * value[2])):
                put(
                    f,
                    j,
                    value[f]
                    + (viscosity * ((east[f] - west[f]) + (north[f] - south[f])) + other),
                )

    def level(k, carry):
        for f in range(4):
            field_copy(f, k).wait()
        for f, ref in enumerate((t_ref, s_ref, u_ref, v_ref)):
            channel = f * levels + k
            parts = [
                (
                    ref[k, :, span] if j < tiles else side_ref[channel],
                    beyond(channel, span),
                )
                for j, span in enumerate(spans)
            ]
            for j in range(count):
                ring(state_ref.at[f, j], *parts[j])
        def put_middle(f, j, value):
            middle_ref[f, j, 8 : 8 + tall] = value
            middle_ref[f, j, 0:8] = value[rows:]

        substep(state_ref, True, tall, put_middle)
        for f in range(4):
            keep_ref[k, f] = middle_ref[f, :, : 8 + tall]
        return carry

    def last_level(k, carry):
        before = jnp.maximum(k - 1, 0)
        above, scale = mix_ref[before], scale_ref[k]
        for f in range(4):
            middle_ref[f, :, : 8 + tall] = keep_ref[k, f]
        solve_ref[0] = jnp.where(k > 0, 1.0, 0.0) * above
        solve_ref[1] = scale

        def put_part(f, j, value):
            span = spans[j]
            before_ref[f, :, span] = (
                value + solve_ref[0, :, span] * before_ref[f, :, span]
            ) * solve_ref[1, :, span]

        substep(middle_ref, False, rows, put_part)
        part_ref[k] = before_ref[...]
        pltpu.make_async_copy(part_ref.at[k], part_out.at[k], out_sem.at[0]).start()
        return carry

    before_ref[...] = jnp.zeros_like(before_ref)
    lax.fori_loop(0, levels, level, 0)
    lax.fori_loop(0, levels, last_level, 0)

    def back(j, solved):
        k = levels - 2 - j
        factor = factor_ref[k]
        return tuple(part_ref[k, f] - factor * solved[f] for f in range(4))

    solved = lax.fori_loop(0, levels - 1, back, tuple(part_ref[levels - 1, f] for f in range(4)))
    for f in range(4):
        top_ref[f] = solved[f]
    pltpu.make_async_copy(part_ref, part_out, out_sem.at[0]).wait()
    factor_copy.wait()
    reply_copy.wait()


def finish_kernel(part_ref, factor_ref, reply_ref, push_ref, t_out, s_out, u_out, v_out):
    levels = t_out.shape[0]
    outs = (t_out, s_out, u_out, v_out)
    last = levels - 1
    for f in range(4):
        outs[f][last] = part_ref[last, f] + push_ref[f] * reply_ref[last]

    def back(j, solved):
        k = last - 1 - j
        factor = factor_ref[k]
        reply = reply_ref[k]
        solved = tuple(part_ref[k, f] - factor * solved[f] for f in range(4))
        for f in range(4):
            outs[f][k] = solved[f] + push_ref[f] * reply
        return solved

    lax.fori_loop(0, last, back, tuple(part_ref[last, f] for f in range(4)))


def per_device(
    atm_flux, send_cell, send_weight, recv_cell, temp, salt, uvel, vvel, wet_mask, vert_mix
):
    levels, block_rows, block_cols = temp.shape
    slot_cells = send_cell[0]
    slot_weights = send_weight[0]
    arrival_cells = recv_cell[0]
    owners, capacity = slot_cells.shape
    atm_cells = atm_flux.shape[1]
    blocks = atm_cells // LANES
    rows = up_to(4 * blocks, 16)
    high = block_rows * block_cols // LANES
    wide = block_cols + EDGE
    columns = lax.axis_size("atm")
    stripes = lax.axis_size("ocn")
    whole = (levels, block_rows, block_cols)
    ocean = (temp, salt, uvel, vvel)

    edge = (5 * HALO, levels * block_rows)
    strips = (4, levels, block_rows, EDGE)
    west, east = call(
        edge_kernel,
        [edge, edge],
        [
            (strips, jnp.float32),
            (strips, jnp.float32),
            ((block_rows, block_cols), jnp.int32),
        ],
        *ocean,
        wet_mask,
        far=5,
        copies=9,
    )
    from_east = lax.ppermute(west, "atm", [((i + 1) % columns, i) for i in range(columns)])
    from_west = lax.ppermute(east, "atm", [(i, (i + 1) % columns) for i in range(columns)])

    strip = (4 * levels + 1, HALO, wide)
    far = pl.BlockSpec(memory_space=pltpu.HBM)
    vmem = pl.BlockSpec(memory_space=pltpu.VMEM)
    main = (4 * levels + 1, HALO, block_cols)
    pair, other = pl.pallas_call(
        strip_kernel,
        out_shape=[jax.ShapeDtypeStruct(strip, jnp.float32)] * 2,
        in_specs=[far] * 5,
        out_specs=[far] * 2,
        scratch_shapes=[
            pltpu.VMEM((4, *whole), jnp.float32),
            pltpu.VMEM((block_rows, block_cols), jnp.int32),
            pltpu.VMEM(main, jnp.float32),
            pltpu.VMEM(main, jnp.float32),
            pltpu.SemaphoreType.DMA((5,)),
            pltpu.SemaphoreType.DMA((10,)),
        ],
        compiler_params=pltpu.CompilerParams(vmem_limit_bytes=VMEM_BYTES),
        cost_estimate=pl.CostEstimate(
            flops=0, transcendentals=0, bytes_accessed=4 * 6 * temp.size
        ),
    )(*ocean, wet_mask)
    side_shape = (4 * levels + 1, block_rows, EDGE)
    pair, other, side = pl.pallas_call(
        side_kernel,
        out_shape=[
            jax.ShapeDtypeStruct(strip, jnp.float32),
            jax.ShapeDtypeStruct(strip, jnp.float32),
            jax.ShapeDtypeStruct(side_shape, jnp.float32),
        ],
        in_specs=[vmem] * 2 + [far] * 2,
        out_specs=[far] * 3,
        scratch_shapes=[
            pltpu.VMEM(side_shape, jnp.float32),
            pltpu.VMEM((4 * levels + 1, HALO, EDGE), jnp.float32),
            pltpu.VMEM((4 * levels + 1, HALO, EDGE), jnp.float32),
            pltpu.SemaphoreType.DMA((3,)),
        ],
        input_output_aliases={2: 0, 3: 1},
        compiler_params=pltpu.CompilerParams(vmem_limit_bytes=SIDE_BYTES),
    )(from_west, from_east, pair, other)
    swaps = [
        [(i + d, i + 1 - d) for i in range(first, stripes - 1, 2) for d in (0, 1)]
        for first in (0, 1)
    ]
    south = lax.ppermute(other, "ocn", swaps[1])
    north = lax.ppermute(pair, "ocn", swaps[0])
    last = stripes - 1
    fold = lax.ppermute(
        other if last % 2 else pair,
        ("atm", "ocn"),
        [(i * stripes + last, (columns - 1 - i) * stripes + last) for i in range(columns)],
    )
    (outgoing,) = call(
        send_kernel,
        [(owners, 4, capacity)],
        [
            (atm_flux.shape, jnp.float32),
            (slot_cells.shape, jnp.int32),
            (slot_cells.shape, jnp.float32),
            ((rows, LANES), jnp.float32),
            ((TERMS * rows, LANES), jnp.bfloat16),
        ],
        atm_flux,
        slot_cells,
        slot_weights,
        far=3,
        copies=3,
        flops=2 * TERMS * rows * LANES * owners * capacity,
    )
    outgoing, north, south, fold = lax.optimization_barrier((outgoing, north, south, fold))
    incoming = lax.all_to_all(outgoing, ("atm", "ocn"), split_axis=0, concat_axis=0, tiled=True)
    (inverse,) = call(
        weight_kernel,
        [(up_to(blocks, 16), LANES)],
        [((TERMS * up_to(blocks, 16), LANES), jnp.float32)],
        slot_cells,
        slot_weights,
        limit=SMALL_BYTES,
        flops=2 * TERMS * up_to(blocks, 16) * LANES * owners * capacity,
    )
    tall = block_rows + 8
    tiles = wide // EDGE
    plane = (block_rows, block_cols)
    shapes = [(levels, 4, *plane), whole, whole, (5, *plane)]
    part, factor, reply, top = pl.pallas_call(
        functools.partial(ocean_kernel, block_rows * stripes),
        out_shape=[jax.ShapeDtypeStruct(shape, jnp.float32) for shape in shapes],
        in_specs=[far] * 10,
        out_specs=[far] * 3 + [vmem],
        scratch_shapes=[
            *[pltpu.VMEM(whole, jnp.float32)] * 4,
            pltpu.VMEM(plane, jnp.int32),
            pltpu.VMEM(side.shape, jnp.float32),
            pltpu.VMEM(strip, jnp.float32),
            pltpu.VMEM(strip, jnp.float32),
            pltpu.VMEM(strip, jnp.float32),
            pltpu.VMEM(vert_mix.shape, jnp.float32),
            pltpu.VMEM(shapes[0], jnp.float32),
            pltpu.VMEM(whole, jnp.float32),
            pltpu.VMEM(whole, jnp.float32),
            pltpu.VMEM(whole, jnp.float32),
            pltpu.VMEM((tiles, tall, EDGE), jnp.float32),
            pltpu.VMEM((tiles, tall + 16, EDGE), jnp.float32),
            pltpu.VMEM((tiles, tall, EDGE), jnp.float32),
            pltpu.VMEM((4, tiles, tall + 16, EDGE), jnp.float32),
            pltpu.VMEM((4, tiles, tall + 16, EDGE), jnp.float32),
            pltpu.VMEM((levels, 4, tiles, tall + 8, EDGE), jnp.float32),
            pltpu.VMEM((2, *plane), jnp.float32),
            pltpu.VMEM((4, *plane), jnp.float32),
            pltpu.SemaphoreType.DMA((6,)),
            pltpu.SemaphoreType.DMA((4, levels)),
            pltpu.SemaphoreType.DMA((3,)),
        ],
        compiler_params=pltpu.CompilerParams(vmem_limit_bytes=VMEM_BYTES),
        cost_estimate=pl.CostEstimate(
            flops=80 * 4 * 2 * temp.size, transcendentals=0, bytes_accessed=4 * 13 * temp.size
        ),
    )(*ocean, wet_mask, side, north, fold, south, vert_mix)

    push, leaving = call(
        exchange_kernel,
        [(4, block_rows, block_cols), (owners, 4, capacity)],
        [
            ((TERMS * 4 * high, LANES), jnp.float32),
            ((TERMS * 4 * high, LANES), jnp.bfloat16),
        ],
        incoming,
        arrival_cells,
        top,
        limit=SMALL_BYTES,
        flops=2 * 2 * TERMS * 4 * high * LANES * owners * capacity,
    )
    returning = lax.all_to_all(leaving, ("atm", "ocn"), split_axis=0, concat_axis=0, tiled=True)
    finished = call(finish_kernel, [whole] * 4, [], part, factor, reply, push)
    (atm_surface,) = call(
        return_kernel,
        [(4, atm_cells)],
        [((TERMS * rows, LANES), jnp.float32)],
        returning,
        slot_cells,
        slot_weights,
        inverse,
        limit=SMALL_BYTES,
        flops=2 * TERMS * rows * LANES * owners * capacity,
    )
    return (*finished, atm_surface)


def solution(mesh):
    in_specs = (
        P(None, ("atm", "ocn")),
        P(("atm", "ocn"), None, None),
        P(("atm", "ocn"), None, None),
        P(("atm", "ocn"), None, None),
        P(None, "ocn", "atm"),
        P(None, "ocn", "atm"),
        P(None, "ocn", "atm"),
        P(None, "ocn", "atm"),
        P("ocn", "atm"),
        P(None, "ocn", "atm"),
    )
    out_specs = (
        P(None, "ocn", "atm"),
        P(None, "ocn", "atm"),
        P(None, "ocn", "atm"),
        P(None, "ocn", "atm"),
        P(None, ("atm", "ocn")),
    )
    return jax.shard_map(
        per_device, mesh=mesh, in_specs=in_specs, out_specs=out_specs, check_vma=False
    )
```

```python
import functools
import math

import jax
import jax.numpy as jnp
from jax import lax
from jax.experimental import pallas as pl
from jax.experimental.pallas import tpu as pltpu
from jax.sharding import PartitionSpec as P

courant_scale = 0.05
diffusion = 0.15
viscosity = 0.15
coriolis = 0.1
heat_gain = 0.25
water_gain = 0.25
stress_gain = 0.25


LANES = 256
TERMS = 2
GROUP = 16
VMEM_BYTES = 60 * 2**20
SMALL_BYTES = 24 * 2**20
SIDE_BYTES = 24 * 2**20


def cut(values):
    terms = []
    rest = values
    for term_index in range(TERMS):
        term = rest.astype(jnp.bfloat16)
        terms.append(term)
        if term_index < TERMS - 1:
            rest = rest - term.astype(jnp.float32)
    return terms


def one_hot(positions, count):
    slots = positions.shape[1]
    base = positions - lax.broadcasted_iota(jnp.int32, (8, slots), 0)
    rows = [jnp.where(base == 8 * j, 1.0, 0.0) for j in range(count // 8)]
    return jnp.concatenate(rows, 0).astype(jnp.bfloat16)


def each_owner(owners, body):
    def outer(group, carry):
        body(group)
        return carry

    lax.fori_loop(0, owners // GROUP, outer, 0)


def send_kernel(
    flux_in, cell_in, weight_in, out_ref, flux_ref, cell_ref, weight_ref, raw_ref, table_ref, sem
):
    owners, slots = cell_ref.shape
    copies = [
        pltpu.make_async_copy(flux_in, flux_ref, sem.at[0]),
        pltpu.make_async_copy(cell_in, cell_ref, sem.at[1]),
        pltpu.make_async_copy(weight_in, weight_ref, sem.at[2]),
    ]
    for copy in copies:
        copy.start()
    blocks = flux_ref.shape[1] // LANES
    raw_ref[...] = jnp.zeros_like(raw_ref)
    copies[0].wait()
    for block in range(blocks):
        x = flux_ref[:, block * LANES : (block + 1) * LANES]
        heat = heat_gain * (x[0:1] + x[1:2] + x[2:3] + x[3:4])
        water = water_gain * (x[4:5] - x[5:6])
        raw_ref[4 * block : 4 * block + 4, :] = jnp.concatenate(
            [heat, water, stress_gain * x[6:8]], 0
        )
    rows = raw_ref.shape[0]
    for term_index, term in enumerate(cut(raw_ref[...])):
        table_ref[term_index * rows : (term_index + 1) * rows, :] = term
    copies[1].wait()
    copies[2].wait()

    def body(group):
        first = pl.multiple_of(group * GROUP, GROUP)
        cells = cell_ref[pl.ds(first, GROUP), :]
        weights = weight_ref[pl.ds(first, GROUP), :]
        for k in range(GROUP):
            cell = cells[k : k + 1]
            found = jnp.dot(
                table_ref[...],
                one_hot(cell & (LANES - 1), LANES),
                preferred_element_type=jnp.float32,
            )
            base = cell // LANES - lax.broadcasted_iota(jnp.int32, (8, slots), 0) // 4
            total = jnp.zeros((8, slots), jnp.float32)
            for j in range(rows // 8):
                value = found[8 * j : 8 * j + 8]
                for t in range(1, TERMS):
                    value = value + found[t * rows + 8 * j : t * rows + 8 * j + 8]
                total = total + jnp.where(base == 2 * j, value, 0.0)
            out_ref[first + k] = (total[0:4] + total[4:8]) * weights[k : k + 1]

    each_owner(owners, body)


def exchange_kernel(come_ref, cell_ref, top_ref, push_ref, out_ref, sum_ref, table_ref):
    owners, slots = cell_ref.shape
    rows, cols = top_ref.shape[1:]
    high = rows * cols // LANES
    sum_ref[...] = jnp.zeros_like(sum_ref)

    def add(group):
        first = pl.multiple_of(group * GROUP, GROUP)
        cells = cell_ref[pl.ds(first, GROUP), :]
        for k in range(GROUP):
            cell = cells[k : k + 1]
            col = cell % cols
            spot = (col // LANES) * rows + cell // cols
            mask = lax.broadcasted_iota(jnp.int32, (high, slots), 0) == spot
            left = []
            for term in cut(come_ref[first + k]):
                wide = term.astype(jnp.float32)
                for f in range(4):
                    left.append(jnp.where(mask, wide[f : f + 1], 0.0))
            sum_ref[...] += lax.dot_general(
                jnp.concatenate(left, 0).astype(jnp.bfloat16),
                one_hot(col % LANES, LANES),
                (((1,), (1,)), ((), ())),
                preferred_element_type=jnp.float32,
            )

    each_owner(owners, add)
    for f in range(4):
        for b in range(cols // LANES):
            span = slice(b * LANES, (b + 1) * LANES)
            value = 0.0
            for t in reversed(range(TERMS)):
                at = (t * 4 + f) * high + b * rows
                value = value + sum_ref[at : at + rows, :]
            push_ref[f, :, span] = value
            surface = top_ref[f, :, span] + value * top_ref[4, :, span]
            for t, term in enumerate(cut(surface)):
                at = (t * 4 + f) * high + b * rows
                table_ref[at : at + rows, :] = term

    def pick(group):
        first = pl.multiple_of(group * GROUP, GROUP)
        cells = cell_ref[pl.ds(first, GROUP), :]
        for k in range(GROUP):
            cell = cells[k : k + 1]
            col = cell % cols
            spot = (col // LANES) * rows + cell // cols
            found = jnp.dot(
                table_ref[...],
                one_hot(col % LANES, LANES),
                preferred_element_type=jnp.float32,
            )
            base = spot - lax.broadcasted_iota(jnp.int32, (8, slots), 0)
            masks = [base == 8 * j for j in range(high // 8)]
            picked = []
            for f in range(4):
                total = jnp.zeros((8, slots), jnp.float32)
                for j in range(high // 8):
                    at = f * high + 8 * j
                    value = found[at : at + 8]
                    for t in range(1, TERMS):
                        value = value + found[t * 4 * high + at : t * 4 * high + at + 8]
                    total = total + jnp.where(masks[j], value, 0.0)
                picked.append(jnp.sum(total, axis=0, keepdims=True))
            out_ref[first + k] = jnp.concatenate(picked, 0)

    each_owner(owners, pick)


def weight_kernel(cell_ref, weight_ref, out_ref, sum_ref):
    owners, slots = cell_ref.shape
    high = sum_ref.shape[0] // TERMS
    sum_ref[...] = jnp.zeros_like(sum_ref)

    def body(group):
        first = pl.multiple_of(group * GROUP, GROUP)
        cells = cell_ref[pl.ds(first, GROUP), :]
        weights = weight_ref[pl.ds(first, GROUP), :]
        for k in range(GROUP):
            cell = cells[k : k + 1]
            mask = lax.broadcasted_iota(jnp.int32, (high, slots), 0) == cell // LANES
            left = [
                jnp.where(mask, term.astype(jnp.float32), 0.0)
                for term in cut(weights[k : k + 1])
            ]
            sum_ref[...] += lax.dot_general(
                jnp.concatenate(left, 0).astype(jnp.bfloat16),
                one_hot(cell & (LANES - 1), LANES),
                (((1,), (1,)), ((), ())),
                preferred_element_type=jnp.float32,
            )

    each_owner(owners, body)
    value = 0.0
    for t in reversed(range(TERMS)):
        value = value + sum_ref[t * high : (t + 1) * high, :]
    out_ref[...] = 1.0 / jnp.maximum(value, 1.0)


def return_kernel(come_ref, cell_ref, weight_ref, inverse_ref, out_ref, sum_ref):
    owners, slots = cell_ref.shape
    blocks = out_ref.shape[1] // LANES
    rows = sum_ref.shape[0] // TERMS
    sum_ref[...] = jnp.zeros_like(sum_ref)

    def body(group):
        first = pl.multiple_of(group * GROUP, GROUP)
        cells = cell_ref[pl.ds(first, GROUP), :]
        weights = weight_ref[pl.ds(first, GROUP), :]
        for k in range(GROUP):
            cell = cells[k : k + 1]
            base = cell // LANES - lax.broadcasted_iota(jnp.int32, (8, slots), 0) // 4
            left = []
            for term in cut(come_ref[first + k] * weights[k : k + 1]):
                wide = term.astype(jnp.float32)
                wide = jnp.concatenate([wide, wide], 0)
                for j in range(rows // 8):
                    left.append(jnp.where(base == 2 * j, wide, 0.0))
            sum_ref[...] += lax.dot_general(
                jnp.concatenate(left, 0).astype(jnp.bfloat16),
                one_hot(cell & (LANES - 1), LANES),
                (((1,), (1,)), ((), ())),
                preferred_element_type=jnp.float32,
            )

    each_owner(owners, body)
    for block in range(blocks):
        value = 0.0
        for t in reversed(range(TERMS)):
            at = t * rows + 4 * block
            value = value + sum_ref[at : at + 4, :]
        out_ref[:, block * LANES : (block + 1) * LANES] = (
            value * inverse_ref[block : block + 1, :]
        )


def up_to(count, step):
    return (count + step - 1) // step * step


def call(kernel, out_shapes, scratch, *operands, far=0, copies=0, limit=VMEM_BYTES, flops=0):
    vmem = pl.BlockSpec(memory_space=pltpu.VMEM)
    return pl.pallas_call(
        kernel,
        out_shape=[jax.ShapeDtypeStruct(shape, jnp.float32) for shape in out_shapes],
        in_specs=[pl.BlockSpec(memory_space=pltpu.HBM)] * far + [vmem] * (len(operands) - far),
        scratch_shapes=[pltpu.VMEM(shape, dtype) for shape, dtype in scratch]
        + [pltpu.SemaphoreType.DMA((copies,))] * (copies > 0),
        compiler_params=pltpu.CompilerParams(vmem_limit_bytes=limit),
        cost_estimate=pl.CostEstimate(
            flops=flops,
            transcendentals=0,
            bytes_accessed=sum(x.size * x.dtype.itemsize for x in operands)
            + sum(4 * math.prod(shape) for shape in out_shapes),
        ),
    )(*operands)


HALO = 2
EDGE = 128


def edge_kernel(t_ref, s_ref, u_ref, v_ref, wet_ref, west_ref, east_ref, left, right, wet, sem):
    levels, rows, cols = t_ref.shape
    count = levels * rows
    copies = []
    for f, ref in enumerate((t_ref, s_ref, u_ref, v_ref)):
        copies.append(
            (
                pltpu.make_async_copy(ref.at[:, :, :EDGE], left.at[f], sem.at[2 * f]),
                pltpu.make_async_copy(ref.at[:, :, cols - EDGE :], right.at[f], sem.at[2 * f + 1]),
            )
        )
    copies.append((pltpu.make_async_copy(wet_ref, wet, sem.at[8]),))
    for group in copies:
        for copy in group:
            copy.start()

    def sides(left, right):
        side = lax.broadcasted_iota(jnp.int32, left.shape, 1) < EDGE // 2
        turned = jnp.where(side, left, right).T
        return turned[:HALO], turned[EDGE - HALO :]

    for f in range(4):
        for copy in copies[f]:
            copy.wait()
        west, east = sides(left[f].reshape(count, EDGE), right[f].reshape(count, EDGE))
        west_ref[HALO * f : HALO * f + HALO, :] = west
        east_ref[HALO * f : HALO * f + HALO, :] = east
    copies[4][0].wait()
    west, east = sides(
        wet[:, :EDGE].astype(jnp.float32), wet[:, cols - EDGE :].astype(jnp.float32)
    )
    west_ref[HALO * 4 : HALO * 5, :] = jnp.zeros((HALO, count), jnp.float32)
    east_ref[HALO * 4 : HALO * 5, :] = jnp.zeros((HALO, count), jnp.float32)
    west_ref[HALO * 4 : HALO * 5, :rows] = west
    east_ref[HALO * 4 : HALO * 5, :rows] = east


def send_strips(even, leaving, act):
    def go(swapped):
        for i, (up, down, out, sem) in enumerate(leaving):
            act(pltpu.make_async_copy(up if i % 2 == swapped else down, out, sem))

    @pl.when(even)
    def _():
        go(0)

    @pl.when(jnp.logical_not(even))
    def _():
        go(1)


def strip_kernel(t_in, s_in, u_in, v_in, wet_in, pair_out, next_out,
                 field_ref, wet_ref, down_ref, up_ref, in_sem, out_sem):
    fields, levels, rows, cols = field_ref.shape
    copies = [
        pltpu.make_async_copy(source, field_ref.at[f], in_sem.at[f])
        for f, source in enumerate((t_in, s_in, u_in, v_in))
    ]
    copies.append(pltpu.make_async_copy(wet_in, wet_ref, in_sem.at[fields]))
    for copy in copies:
        copy.start()
    even = lax.axis_index("ocn") % 2 == 0
    leaving = []
    for f in range(fields + 1):
        copies[f].wait()
        if f < fields:
            span = slice(f * levels, (f + 1) * levels)
            down_ref[span] = field_ref[f, :, :HALO, :]
            up_ref[span] = field_ref[f, :, rows - HALO :, :]
        else:
            span = slice(fields * levels, fields * levels + 1)
            wet = wet_ref[...].astype(jnp.float32)
            down_ref[fields * levels] = wet[:HALO]
            up_ref[fields * levels] = wet[rows - HALO :]
        leaving += [
            (up_ref.at[span], down_ref.at[span], out.at[span, :, :cols], out_sem.at[2 * f + i])
            for i, out in enumerate((pair_out, next_out))
        ]
        send_strips(even, leaving[-2:], lambda copy: copy.start())
    send_strips(even, leaving, lambda copy: copy.wait())


def side_kernel(from_west_ref, from_east_ref, pair_in, next_in, pair_out, next_out, side_out,
                side_ref, low_ref, high_ref, sem):
    channels, rows, _ = side_ref.shape
    levels = (channels - 1) // 4
    cols = pair_out.shape[2] - EDGE

    def turned(f, count):
        return jnp.concatenate(
            [
                from_east_ref[HALO * f : HALO * f + HALO, :count],
                jnp.zeros((EDGE - 2 * HALO, count), jnp.float32),
                from_west_ref[HALO * f : HALO * f + HALO, :count],
            ],
            0,
        ).T

    for f in range(4):
        side_ref[f * levels : (f + 1) * levels] = turned(f, levels * rows).reshape(
            levels, rows, EDGE
        )
    side_ref[4 * levels] = turned(4, rows)
    low_ref[...] = side_ref[:, :HALO, :]
    high_ref[...] = side_ref[:, rows - HALO :, :]
    even = lax.axis_index("ocn") % 2 == 0
    leaving = [
        (high_ref, low_ref, out.at[:, :, cols:], sem.at[i])
        for i, out in enumerate((pair_out, next_out))
    ]
    side_copy = pltpu.make_async_copy(side_ref, side_out, sem.at[2])
    side_copy.start()
    send_strips(even, leaving, lambda copy: copy.start())
    side_copy.wait()
    send_strips(even, leaving, lambda copy: copy.wait())


def ocean_kernel(total_rows, t_in, s_in, u_in, v_in, wet_in, side_in, pair_in, fold_in,
                 next_in, mix_in, part_out, factor_out, reply_out, top_ref,
                 t_ref, s_ref, u_ref, v_ref, wet_ref, side_ref, north_ref, fold_ref, south_ref,
                 mix_ref, part_ref, scale_ref, factor_ref, reply_ref, east_gate, north_gate,
                 turn_ref, state_ref, middle_ref, keep_ref, solve_ref, before_ref, in_sem, level_sem, out_sem):
    levels, rows, cols = t_ref.shape
    tall = rows + 8
    tiles = cols // EDGE
    spans = [slice(j * EDGE, (j + 1) * EDGE) for j in range(tiles + 1)]
    stripe = lax.axis_index("ocn")
    on_top = stripe == lax.axis_size("ocn") - 1
    copies = [
        pltpu.make_async_copy(source, target, in_sem.at[i])
        for i, (source, target) in enumerate(
            (
                (mix_in, mix_ref),
                (wet_in, wet_ref),
                (side_in, side_ref),
            )
        )
    ]
    fold_copy = pltpu.make_async_copy(fold_in, fold_ref, in_sem.at[5])
    even = stripe % 2 == 0
    strips = [
        (north_ref, south_ref, source, in_sem.at[3 + i])
        for i, source in enumerate((pair_in, next_in))
    ]

    def take_strips(swapped, act):
        for i, (north, south, source, sem) in enumerate(strips):
            act(pltpu.make_async_copy(source, north if i == swapped else south, sem))

    for copy in copies[:2]:
        copy.start()

    @pl.when(even)
    def _():
        take_strips(0, lambda copy: copy.start())

    @pl.when(jnp.logical_not(even))
    def _():
        take_strips(1, lambda copy: copy.start())

    @pl.when(on_top)
    def _():
        fold_copy.start()

    copies[2].start()

    def field_copy(f, k):
        source, target = ((t_in, t_ref), (s_in, s_ref), (u_in, u_ref), (v_in, v_ref))[f]
        return pltpu.make_async_copy(source.at[k], target.at[k], level_sem.at[f, k])

    def fetch(k, carry):
        for f in range(4):
            field_copy(f, k).start()
        return carry

    lax.fori_loop(0, levels, fetch, 0)

    copies[0].wait()
    above = jnp.zeros((rows, cols), jnp.float32)
    factor = above
    reply = None
    for k in range(levels):
        below = mix_ref[k] if k < levels - 1 else jnp.zeros_like(above)
        scale = 1.0 / (1.0 + above + below + above * factor)
        factor = -below * scale
        reply = scale if k == 0 else above * reply * scale
        scale_ref[k] = scale
        factor_ref[k] = factor
        reply_ref[k] = reply
        above = below
    factor_copy = pltpu.make_async_copy(factor_ref, factor_out, out_sem.at[1])
    factor_copy.start()
    copies[1].wait()
    open_water = wet_ref[...].astype(jnp.float32)
    for k in range(levels - 2, -1, -1):
        reply_ref[k + 1] = reply * open_water
        reply = reply_ref[k] - factor_ref[k] * reply
    reply_ref[0] = reply * open_water
    top_ref[4] = reply * open_water
    reply_copy = pltpu.make_async_copy(reply_ref, reply_out, out_sem.at[2])
    reply_copy.start()
    for copy in copies[2:]:
        copy.wait()

    @pl.when(even)
    def _():
        take_strips(0, lambda copy: copy.wait())

    @pl.when(jnp.logical_not(even))
    def _():
        take_strips(1, lambda copy: copy.wait())

    @pl.when(on_top)
    def _():
        fold_copy.wait()
        flip = EDGE - 1 - lax.broadcasted_iota(jnp.int32, (8, EDGE), 1)
        order = list(range(tiles))[::-1] + [tiles]
        blank = jnp.zeros((8 - HALO, EDGE), jnp.float32)

        def mirror(channel, sign):
            fold = fold_ref[channel]
            for j, span in enumerate(spans):
                part = fold[:, spans[order[j]]]
                part = jnp.concatenate([part[1:2], part[0:1], blank], 0)
                part = jnp.take_along_axis(part, flip, axis=1)
                north_ref[channel, :, span] = part[:HALO] * sign

        def mirror_level(k, carry):
            for f in range(4):
                mirror(f * levels + k, 1.0 if f < 2 else -1.0)
            return carry

        lax.fori_loop(0, levels, mirror_level, 0, unroll=4)
        mirror(4 * levels, 1.0)

    gap = jnp.zeros((8 - 2 * HALO, EDGE), jnp.float32)

    def beyond(channel, span):
        return jnp.concatenate([north_ref[channel, :, span], gap, south_ref[channel, :, span]], 0)

    lane = lax.broadcasted_iota(jnp.int32, (tall, EDGE), 1)
    first = lane == 0
    final = lane == EDGE - 1
    count = tiles + 1

    def ring(ref, centre, outer):
        ref[8 : 8 + rows] = centre
        ref[8 + rows : 8 + tall] = outer
        ref[0:8] = outer
        ref[8 + tall : 16 + tall] = centre[0:8]

    def ahead(x):
        return pltpu.roll(x, EDGE - 1, 1)

    def behind(x):
        return pltpu.roll(x, 1, 1)

    row = lax.broadcasted_iota(jnp.int32, (tall, EDGE), 0)
    row = jnp.where(row >= tall - HALO, row - tall, row) + stripe * rows
    row = jnp.where(row >= total_rows, 2 * total_rows - 1 - row, row)
    latitude = jnp.pi * ((row.astype(jnp.float32) + 0.5) / total_rows - 0.5)
    turn = coriolis * jnp.sin(latitude)
    for j, span in enumerate(spans):
        ring(
            state_ref.at[0, j],
            open_water[:, span] if j < tiles else side_ref[4 * levels],
            beyond(4 * levels, span),
        )
    for j in range(count):
        wet = state_ref[0, j, 8 : 8 + tall]
        after = state_ref[0, (j + 1) % count, 8 : 8 + tall]
        east_gate[j] = wet * jnp.where(final, ahead(after), ahead(wet))
        north = wet * state_ref[0, j, 9 : 9 + tall]
        ring(north_gate.at[j], north[:rows], north[rows:])
        turn_ref[j] = turn * wet

    def substep(source, closed, height, put):
        def rolled(j):
            return [ahead(source[f, j, 8 : 8 + height]) for f in range(4)]

        def eastward(j, here, after):
            gate = east_gate[j, :height]
            return [
                gate
                * (jnp.where(final[:height], after[f], here[f]) - source[f, j, 8 : 8 + height])
                for f in range(4)
            ]

        here = rolled(0)
        side = rolled(tiles)
        side_east = eastward(tiles, side, here)
        passed = [behind(x) for x in side_east]
        for j in range(count if closed else tiles):
            if j < tiles:
                after = rolled(j + 1) if j + 1 < tiles else side
                east = eastward(j, here, after)
            else:
                after, east = None, side_east
            here = after
            before = passed
            passed = [behind(x) for x in east]
            west = [jnp.where(first[:height], p, q) for p, q in zip(before, passed)]
            north_open = north_gate[j, 8 : 8 + height]
            south_open = north_gate[j, 7 : 7 + height]
            value = [source[f, j, 8 : 8 + height] for f in range(4)]
            north = [
                north_open * (source[f, j, 9 : 9 + height] - value[f]) for f in range(4)
            ]
            south = [
                south_open * (value[f] - source[f, j, 7 : 7 + height]) for f in range(4)
            ]
            cx = courant_scale * value[2]
            cy = courant_scale * value[3]
            to_east = diffusion - jnp.minimum(cx, 0.0)
            to_west = diffusion + jnp.maximum(cx, 0.0)
            to_north = diffusion - jnp.minimum(cy, 0.0)
            to_south = diffusion + jnp.maximum(cy, 0.0)
            for f in range(2):
                put(
                    f,
                    j,
                    value[f]
                    + (
                        (to_east * east[f] - to_west * west[f])
                        + (to_north * north[f] - to_south * south[f])
                    ),
                )
            turning = turn_ref[j, :height]
            for f, other in ((2, turning * value[3]), (3, -turning * value[2])):
                put(
                    f,
                    j,
                    value[f]
                    + (viscosity * ((east[f] - west[f]) + (north[f] - south[f])) + other),
                )

    def level(k, carry):
        for f in range(4):
            field_copy(f, k).wait()
        for f, ref in enumerate((t_ref, s_ref, u_ref, v_ref)):
            channel = f * levels + k
            parts = [
                (
                    ref[k, :, span] if j < tiles else side_ref[channel],
                    beyond(channel, span),
                )
                for j, span in enumerate(spans)
            ]
            for j in range(count):
                ring(state_ref.at[f, j], *parts[j])
        def put_middle(f, j, value):
            middle_ref[f, j, 8 : 8 + tall] = value
            middle_ref[f, j, 0:8] = value[rows:]

        substep(state_ref, True, tall, put_middle)
        for f in range(4):
            keep_ref[k, f] = middle_ref[f, :, : 8 + tall]
        return carry

    def last_level(k, carry):
        before = jnp.maximum(k - 1, 0)
        above, scale = mix_ref[before], scale_ref[k]
        for f in range(4):
            middle_ref[f, :, : 8 + tall] = keep_ref[k, f]
        solve_ref[0] = jnp.where(k > 0, 1.0, 0.0) * above
        solve_ref[1] = scale

        def put_part(f, j, value):
            span = spans[j]
            before_ref[f, :, span] = (
                value + solve_ref[0, :, span] * before_ref[f, :, span]
            ) * solve_ref[1, :, span]

        substep(middle_ref, False, rows, put_part)
        part_ref[k] = before_ref[...]
        pltpu.make_async_copy(part_ref.at[k], part_out.at[k], out_sem.at[0]).start()
        return carry

    before_ref[...] = jnp.zeros_like(before_ref)
    lax.fori_loop(0, levels, level, 0)
    lax.fori_loop(0, levels, last_level, 0)

    def back(j, solved):
        k = levels - 2 - j
        factor = factor_ref[k]
        return tuple(part_ref[k, f] - factor * solved[f] for f in range(4))

    solved = lax.fori_loop(0, levels - 1, back, tuple(part_ref[levels - 1, f] for f in range(4)))
    for f in range(4):
        top_ref[f] = solved[f]
    pltpu.make_async_copy(part_ref, part_out, out_sem.at[0]).wait()
    factor_copy.wait()
    reply_copy.wait()


def finish_kernel(part_ref, factor_ref, reply_ref, push_ref, t_out, s_out, u_out, v_out):
    levels = t_out.shape[0]
    outs = (t_out, s_out, u_out, v_out)
    last = levels - 1
    for f in range(4):
        outs[f][last] = part_ref[last, f] + push_ref[f] * reply_ref[last]

    def back(j, solved):
        k = last - 1 - j
        factor = factor_ref[k]
        reply = reply_ref[k]
        solved = tuple(part_ref[k, f] - factor * solved[f] for f in range(4))
        for f in range(4):
            outs[f][k] = solved[f] + push_ref[f] * reply
        return solved

    lax.fori_loop(0, last, back, tuple(part_ref[last, f] for f in range(4)))


def per_device(
    atm_flux, send_cell, send_weight, recv_cell, temp, salt, uvel, vvel, wet_mask, vert_mix
):
    levels, block_rows, block_cols = temp.shape
    slot_cells = send_cell[0]
    slot_weights = send_weight[0]
    arrival_cells = recv_cell[0]
    owners, capacity = slot_cells.shape
    atm_cells = atm_flux.shape[1]
    blocks = atm_cells // LANES
    rows = up_to(4 * blocks, 16)
    high = block_rows * block_cols // LANES
    wide = block_cols + EDGE
    columns = lax.axis_size("atm")
    stripes = lax.axis_size("ocn")
    whole = (levels, block_rows, block_cols)
    ocean = (temp, salt, uvel, vvel)

    edge = (5 * HALO, levels * block_rows)
    strips = (4, levels, block_rows, EDGE)
    west, east = call(
        edge_kernel,
        [edge, edge],
        [
            (strips, jnp.float32),
            (strips, jnp.float32),
            ((block_rows, block_cols), jnp.int32),
        ],
        *ocean,
        wet_mask,
        far=5,
        copies=9,
    )
    from_east = lax.ppermute(west, "atm", [((i + 1) % columns, i) for i in range(columns)])
    from_west = lax.ppermute(east, "atm", [(i, (i + 1) % columns) for i in range(columns)])

    strip = (4 * levels + 1, HALO, wide)
    far = pl.BlockSpec(memory_space=pltpu.HBM)
    vmem = pl.BlockSpec(memory_space=pltpu.VMEM)
    main = (4 * levels + 1, HALO, block_cols)
    pair, other = pl.pallas_call(
        strip_kernel,
        out_shape=[jax.ShapeDtypeStruct(strip, jnp.float32)] * 2,
        in_specs=[far] * 5,
        out_specs=[far] * 2,
        scratch_shapes=[
            pltpu.VMEM((4, *whole), jnp.float32),
            pltpu.VMEM((block_rows, block_cols), jnp.int32),
            pltpu.VMEM(main, jnp.float32),
            pltpu.VMEM(main, jnp.float32),
            pltpu.SemaphoreType.DMA((5,)),
            pltpu.SemaphoreType.DMA((10,)),
        ],
        compiler_params=pltpu.CompilerParams(vmem_limit_bytes=VMEM_BYTES),
        cost_estimate=pl.CostEstimate(
            flops=0, transcendentals=0, bytes_accessed=4 * 6 * temp.size
        ),
    )(*ocean, wet_mask)
    side_shape = (4 * levels + 1, block_rows, EDGE)
    pair, other, side = pl.pallas_call(
        side_kernel,
        out_shape=[
            jax.ShapeDtypeStruct(strip, jnp.float32),
            jax.ShapeDtypeStruct(strip, jnp.float32),
            jax.ShapeDtypeStruct(side_shape, jnp.float32),
        ],
        in_specs=[vmem] * 2 + [far] * 2,
        out_specs=[far] * 3,
        scratch_shapes=[
            pltpu.VMEM(side_shape, jnp.float32),
            pltpu.VMEM((4 * levels + 1, HALO, EDGE), jnp.float32),
            pltpu.VMEM((4 * levels + 1, HALO, EDGE), jnp.float32),
            pltpu.SemaphoreType.DMA((3,)),
        ],
        input_output_aliases={2: 0, 3: 1},
        compiler_params=pltpu.CompilerParams(vmem_limit_bytes=SIDE_BYTES),
    )(from_west, from_east, pair, other)
    swaps = [
        [(i + d, i + 1 - d) for i in range(first, stripes - 1, 2) for d in (0, 1)]
        for first in (0, 1)
    ]
    south = lax.ppermute(other, "ocn", swaps[1])
    north = lax.ppermute(pair, "ocn", swaps[0])
    last = stripes - 1
    fold = lax.ppermute(
        other if last % 2 else pair,
        ("atm", "ocn"),
        [(i * stripes + last, (columns - 1 - i) * stripes + last) for i in range(columns)],
    )
    (outgoing,) = call(
        send_kernel,
        [(owners, 4, capacity)],
        [
            (atm_flux.shape, jnp.float32),
            (slot_cells.shape, jnp.int32),
            (slot_cells.shape, jnp.float32),
            ((rows, LANES), jnp.float32),
            ((TERMS * rows, LANES), jnp.bfloat16),
        ],
        atm_flux,
        slot_cells,
        slot_weights,
        far=3,
        copies=3,
        flops=2 * TERMS * rows * LANES * owners * capacity,
    )
    outgoing, north, south, fold = lax.optimization_barrier((outgoing, north, south, fold))
    incoming = lax.all_to_all(outgoing, ("atm", "ocn"), split_axis=0, concat_axis=0, tiled=True)
    (inverse,) = call(
        weight_kernel,
        [(up_to(blocks, 16), LANES)],
        [((TERMS * up_to(blocks, 16), LANES), jnp.float32)],
        slot_cells,
        slot_weights,
        limit=SMALL_BYTES,
        flops=2 * TERMS * up_to(blocks, 16) * LANES * owners * capacity,
    )
    tall = block_rows + 8
    tiles = wide // EDGE
    plane = (block_rows, block_cols)
    shapes = [(levels, 4, *plane), whole, whole, (5, *plane)]
    part, factor, reply, top = pl.pallas_call(
        functools.partial(ocean_kernel, block_rows * stripes),
        out_shape=[jax.ShapeDtypeStruct(shape, jnp.float32) for shape in shapes],
        in_specs=[far] * 10,
        out_specs=[far] * 3 + [vmem],
        scratch_shapes=[
            *[pltpu.VMEM(whole, jnp.float32)] * 4,
            pltpu.VMEM(plane, jnp.int32),
            pltpu.VMEM(side.shape, jnp.float32),
            pltpu.VMEM(strip, jnp.float32),
            pltpu.VMEM(strip, jnp.float32),
            pltpu.VMEM(strip, jnp.float32),
            pltpu.VMEM(vert_mix.shape, jnp.float32),
            pltpu.VMEM(shapes[0], jnp.float32),
            pltpu.VMEM(whole, jnp.float32),
            pltpu.VMEM(whole, jnp.float32),
            pltpu.VMEM(whole, jnp.float32),
            pltpu.VMEM((tiles, tall, EDGE), jnp.float32),
            pltpu.VMEM((tiles, tall + 16, EDGE), jnp.float32),
            pltpu.VMEM((tiles, tall, EDGE), jnp.float32),
            pltpu.VMEM((4, tiles, tall + 16, EDGE), jnp.float32),
            pltpu.VMEM((4, tiles, tall + 16, EDGE), jnp.float32),
            pltpu.VMEM((levels, 4, tiles, tall + 8, EDGE), jnp.float32),
            pltpu.VMEM((2, *plane), jnp.float32),
            pltpu.VMEM((4, *plane), jnp.float32),
            pltpu.SemaphoreType.DMA((6,)),
            pltpu.SemaphoreType.DMA((4, levels)),
            pltpu.SemaphoreType.DMA((3,)),
        ],
        compiler_params=pltpu.CompilerParams(vmem_limit_bytes=VMEM_BYTES),
        cost_estimate=pl.CostEstimate(
            flops=80 * 4 * 2 * temp.size, transcendentals=0, bytes_accessed=4 * 13 * temp.size
        ),
    )(*ocean, wet_mask, side, north, fold, south, vert_mix)

    push, leaving = call(
        exchange_kernel,
        [(4, block_rows, block_cols), (owners, 4, capacity)],
        [
            ((TERMS * 4 * high, LANES), jnp.float32),
            ((TERMS * 4 * high, LANES), jnp.bfloat16),
        ],
        incoming,
        arrival_cells,
        top,
        limit=SMALL_BYTES,
        flops=2 * 2 * TERMS * 4 * high * LANES * owners * capacity,
    )
    returning = lax.all_to_all(leaving, ("atm", "ocn"), split_axis=0, concat_axis=0, tiled=True)
    finished = call(finish_kernel, [whole] * 4, [], part, factor, reply, push)
    (atm_surface,) = call(
        return_kernel,
        [(4, atm_cells)],
        [((TERMS * rows, LANES), jnp.float32)],
        returning,
        slot_cells,
        slot_weights,
        inverse,
        limit=SMALL_BYTES,
        flops=2 * TERMS * rows * LANES * owners * capacity,
    )
    return (*finished, atm_surface)


def solution(mesh):
    in_specs = (
        P(None, ("atm", "ocn")),
        P(("atm", "ocn"), None, None),
        P(("atm", "ocn"), None, None),
        P(("atm", "ocn"), None, None),
        P(None, "ocn", "atm"),
        P(None, "ocn", "atm"),
        P(None, "ocn", "atm"),
        P(None, "ocn", "atm"),
        P("ocn", "atm"),
        P(None, "ocn", "atm"),
    )
    out_specs = (
        P(None, "ocn", "atm"),
        P(None, "ocn", "atm"),
        P(None, "ocn", "atm"),
        P(None, "ocn", "atm"),
        P(None, ("atm", "ocn")),
    )
    return jax.shard_map(
        per_device, mesh=mesh, in_specs=in_specs, out_specs=out_specs, check_vma=False
    )
```
